32 devices in a mesh: dp: 8 (over y, x, core), seq: 4 (over z).
Axes of the slice: x: 2, y: 2, z: 4, core: 2. Of those that a mesh axis runs over, the one named last changes fastest.
Arguments:
- layer_input: bfloat16 [8, 2048, 768], P('dp', 'seq'), may hold values from -6 to 6
- cotangent: bfloat16 [8, 2048, 768], P('dp', 'seq'), may hold values from -6 to 6
- segment_ids: int32 [8, 2048], P('dp', 'seq'), may hold values from 0 to 8, as said below
- route_index: int32 [8, 3, 256], P('dp'), may hold values from 0 to 2047, as said below
- route_count: int32 [8, 3], P('dp'), may hold values from 128 to 256, as said below
- attn_gain: bfloat16 [768], P(('dp', 'seq')), may hold values from 0.5 to 1.5
- light_qkv: bfloat16 [768, 2304], P(('dp', 'seq')), may hold values from -0.21875 to 0.21875
- light_out: bfloat16 [768, 768], P(('dp', 'seq')), may hold values from -0.875 to 0.875
- heavy_qkv: bfloat16 [768, 2304], P(('dp', 'seq')), may hold values from -0.21875 to 0.21875
- heavy_out: bfloat16 [768, 768], P(('dp', 'seq')), may hold values from -0.875 to 0.875
- attn_router: bfloat16 [768], P(('dp', 'seq')), may hold values from -0.21875 to 0.21875
- ffn_gain: bfloat16 [768], P(('dp', 'seq')), may hold values from 0.5 to 1.5
- light_gate_up: bfloat16 [768, 2048], P(('dp', 'seq')), may hold values from -0.21875 to 0.21875
- light_down: bfloat16 [1024, 768], P(('dp', 'seq')), may hold values from -0.1875 to 0.1875
- heavy_gate_up: bfloat16 [768, 8192], P(('dp', 'seq')), may hold values from -0.21875 to 0.21875
- heavy_down: bfloat16 [4096, 768], P(('dp', 'seq')), may hold values from -0.1875 to 0.1875
- ffn_router: bfloat16 [768], P(('dp', 'seq')), may hold values from -0.21875 to 0.21875
Outputs:
- layer_output: bfloat16 [8, 2048, 768], P('dp', 'seq')
- input_grad: bfloat16 [8, 2048, 768], P('dp', 'seq')
- grad_attn_gain: float32 [768], P(('dp', 'seq'))
- grad_light_qkv: float32 [768, 2304], P(('dp', 'seq'))
- grad_light_out: float32 [768, 768], P(('dp', 'seq'))
- grad_heavy_qkv: float32 [768, 2304], P(('dp', 'seq'))
- grad_heavy_out: float32 [768, 768], P(('dp', 'seq'))
- grad_attn_router: float32 [768], P(('dp', 'seq'))
- grad_ffn_gain: float32 [768], P(('dp', 'seq'))
- grad_light_gate_up: float32 [768, 2048], P(('dp', 'seq'))
- grad_light_down: float32 [1024, 768], P(('dp', 'seq'))
- grad_heavy_gate_up: float32 [768, 8192], P(('dp', 'seq'))
- grad_heavy_down: float32 [4096, 768], P(('dp', 'seq'))
- grad_ffn_router: float32 [768], P(('dp', 'seq'))
The draws below stay inside these ranges and needn't reach their ends.
Inputs may be any that keep to these rules, and one draw needn't show every extreme that they name: `segment_ids`: segment ids never fall along a row; in each row one segment begins within the first 512 tokens and ends within the last 512. `route_index`: for each row and set the first route_count slots hold distinct positions of the row in increasing order, later slots repeat the first position; every position of set 0 is also a position of set 1. `route_count`: in every draw each set has 256 live slots in some row; a row's count of set 1 is at least its count of set 0.
All inputs are finite; a program needn't handle non-finite values.
Results may differ from the reference program's by a relative error of at most 0.017.
Values may be sent and summed in bfloat16 or wider, within the bound.
No kernel may reach another device: no remote copies, remote signals or barrier semaphores. Data moves between devices by JAX's collectives and lax.ppermute only.
A program may use at most 256 MiB of HBM per device.

```python
import jax
import jax.numpy as jnp
from jax import lax

D = 768
L_HEADS = 8
L_HEAD = 96
H_HEADS = 12
H_HEAD = 64
LFF = 1024
HFF = 4096
WINDOW = 128
TOK_DEV = 512
LIGHT_INNER = 768
HEAVY_INNER = 768
ROW_LEN = 2048
ROWS = 8
ROUTED = 256


def draw_segment_ids(key, part):
    cut_keys = jax.random.split(key, 4)
    start_cut = jax.random.randint(cut_keys[0], (ROWS, 1), 1, TOK_DEV)
    end_cut = ROW_LEN - jax.random.randint(cut_keys[1], (ROWS, 1), 1, TOK_DEV)
    early_cuts = jnp.minimum(jax.random.randint(cut_keys[2], (ROWS, 3), 1, TOK_DEV), start_cut)
    late_cuts = jnp.maximum(ROW_LEN - jax.random.randint(cut_keys[3], (ROWS, 3), 1, TOK_DEV), end_cut)
    all_cuts = jnp.concatenate([early_cuts, start_cut, end_cut, late_cuts], axis=1)
    position = jnp.arange(ROW_LEN, dtype=jnp.int32)
    passed = (all_cuts[:, None, :] <= position[None, :, None]).astype(jnp.int32)
    return jnp.sum(passed, axis=2).astype(jnp.int32)


def permuted_rows(key):
    row_keys = jax.random.split(key, ROWS)
    return jax.vmap(lambda one_key: jax.random.permutation(one_key, ROW_LEN))(row_keys)


def route_ranks(key):
    order_key, weight_key = jax.random.split(key)
    shuffled = permuted_rows(order_key).astype(jnp.int32)
    stretch_weight = jax.random.randint(weight_key, (ROWS, ROW_LEN // TOK_DEV), 1, 4)
    stretch_of = jnp.broadcast_to(jnp.arange(ROW_LEN, dtype=jnp.int32) // TOK_DEV, (ROWS, ROW_LEN))
    weighted = shuffled * jnp.take_along_axis(stretch_weight, stretch_of, axis=1) * ROW_LEN + shuffled
    return jnp.argsort(jnp.argsort(weighted, axis=1, stable=True), axis=1, stable=True).astype(jnp.int32)


def slot_list(rank_row, live_count):
    position = jnp.arange(ROW_LEN, dtype=jnp.int32)
    chosen = rank_row < live_count[:, None]
    sort_key = jnp.where(chosen, position[None, :], ROW_LEN + position[None, :])
    listed = jnp.argsort(sort_key, axis=1, stable=True)[:, :ROUTED].astype(jnp.int32)
    is_live = jnp.arange(ROUTED)[None, :] < live_count[:, None]
    return jnp.where(is_live, listed, listed[:, :1])


def route_plan(key):
    plan_keys = jax.random.split(jax.random.fold_in(key, 11), 4)
    shortfall = jax.random.randint(plan_keys[0], (ROWS, 3), 0, ROUTED // 2 + 1)
    full_row = jax.random.randint(plan_keys[1], (1, 3), 0, ROWS)
    counts = jnp.where(jnp.arange(ROWS)[:, None] == full_row, ROUTED, ROUTED - shortfall)
    counts = jnp.stack([counts[:, 0], jnp.maximum(counts[:, 0], counts[:, 1]), counts[:, 2]], axis=1).astype(jnp.int32)
    attention_rank = route_ranks(plan_keys[2])
    ffn_rank = route_ranks(plan_keys[3])
    slot_index = jnp.stack([slot_list(attention_rank, counts[:, 0]), slot_list(attention_rank, counts[:, 1]), slot_list(ffn_rank, counts[:, 2])], axis=1)
    return (slot_index.astype(jnp.int32), counts)


def draw_route_index(key, part):
    return route_plan(key)[0]


def draw_route_count(key, part):
    return route_plan(key)[1]


def spiked(result, own_key, source, target, shards_of, factor):
    owner, partner = [(jnp.arange(result.shape[dim]) // (result.shape[dim] // shards_of)).reshape([-1 if axis == dim else 1 for axis in range(result.ndim)]) for dim in (source, target)]
    chosen = jax.random.permutation(own_key, shards_of)[partner]
    strong = (owner == chosen) | (owner == (partner + shards_of // 2) % shards_of)
    return jnp.where(strong, factor * result, result)


def block_levels(rng, extent, cuts, least, high):
    gain, own = 1.0, jax.random.fold_in(rng, 6)
    for dim, shards_of in cuts:
        draws = jnp.exp(jax.random.uniform(jax.random.fold_in(own, dim), (shards_of,), jnp.float32, least / len(cuts), high / len(cuts)))
        gain = gain * jnp.repeat(draws, extent[dim] // shards_of).reshape([-1 if axis == dim else 1 for axis in range(len(extent))])
    return gain


def bell_draw(stream_key, shape, deviation, limit, pieces=(), held_as=jnp.bfloat16):
    array = deviation * jax.random.normal(stream_key, shape, jnp.float32)
    if pieces:
        array = array * block_levels(stream_key, shape, pieces, -0.22, 0.18)
    return jnp.clip(array, -limit, limit).astype(held_as)


def bell_draw_with(rng, shape, deviation, most, shards, heavy, kind=jnp.bfloat16):
    array = deviation * jax.random.normal(rng, shape, jnp.float32)
    if shards:
        array = array * block_levels(rng, shape, shards, -0.22, 0.18)
    return jnp.clip(spiked(array, jax.random.fold_in(rng, 3), *heavy), -most, most).astype(kind)


def setup_inputs(seed: int = 0) -> dict:
    splits = jax.random.split(jax.random.key(seed), 18)
    layer_input = bell_draw(splits[0], (ROWS, ROW_LEN, D), 1.0, 6.0, ((0, 8), (1, 4)))
    cotangent = bell_draw_with(splits[1], (ROWS, ROW_LEN, D), 1.0, 6.0, ((0, 8), (1, 4)), (1, 2, 4, 2.0))
    segment_ids = draw_segment_ids(jax.random.fold_in(splits[17], 71), 0)
    route_index = draw_route_index(jax.random.fold_in(splits[17], 71), 0)
    route_count = draw_route_count(jax.random.fold_in(splits[17], 71), 0)
    attn_gain = jnp.clip(1.0 + 0.1 * jax.random.normal(splits[5], (D,), jnp.float32), 0.5, 1.5).astype(jnp.bfloat16)
    light_qkv = bell_draw(splits[6], (D, 3 * LIGHT_INNER), D ** -0.5, 0.21875, ((0, 32),))
    light_out = bell_draw(splits[7], (LIGHT_INNER, D), (LIGHT_INNER // 16) ** -0.5, 0.875, ((0, 32),))
    heavy_qkv = bell_draw(splits[8], (D, 3 * HEAVY_INNER), D ** -0.5, 0.21875, ((0, 32),))
    heavy_out = bell_draw(splits[9], (HEAVY_INNER, D), (HEAVY_INNER // 16) ** -0.5, 0.875, ((0, 32),))
    attn_router = bell_draw(splits[10], (D,), D ** -0.5, 0.21875, ((0, 32),))
    ffn_gain = jnp.clip(1.0 + 0.1 * jax.random.normal(splits[11], (D,), jnp.float32), 0.5, 1.5).astype(jnp.bfloat16)
    light_gate_up = bell_draw(splits[12], (D, 2 * LFF), D ** -0.5, 0.21875, ((0, 32),))
    light_down = bell_draw(splits[13], (LFF, D), LFF ** -0.5, 0.1875, ((0, 32),))
    heavy_gate_up = bell_draw(splits[14], (D, 2 * HFF), D ** -0.5, 0.21875, ((0, 32),))
    heavy_down = bell_draw(splits[15], (HFF, D), (HFF // 4) ** -0.5, 0.1875, ((0, 32),))
    ffn_router = bell_draw(splits[16], (D,), D ** -0.5, 0.21875, ((0, 32),))
    return {"layer_input": layer_input, "cotangent": cotangent, "segment_ids": segment_ids, "route_index": route_index, "route_count": route_count, "attn_gain": attn_gain, "light_qkv": light_qkv, "light_out": light_out, "heavy_qkv": heavy_qkv, "heavy_out": heavy_out, "attn_router": attn_router, "ffn_gain": ffn_gain, "light_gate_up": light_gate_up, "light_down": light_down, "heavy_gate_up": heavy_gate_up, "heavy_down": heavy_down, "ffn_router": ffn_router}


@jax.custom_vjp
def low(v):
    return lax.optimization_barrier(v.astype(jnp.bfloat16)).astype(jnp.float32)

@jax.custom_vjp
def low_back(v):
    return v

def low_keep(v):
    return (low(v), None)

def low_pass(kept, grad):
    return (grad,)

def back_keep(v):
    return (v, None)

def back_low(kept, grad):
    return (low(grad),)
low.defvjp(low_keep, low_pass)
low_back.defvjp(back_keep, back_low)
epsilon = 1e-06
masked_score = -1e+30
gelu_scale = 0.7978845608028654
highest = lax.Precision.HIGHEST

def both_ways(values):
    return low_back(low(values))

def product(left_side, right_side):
    return jnp.dot(left_side, right_side, precision=highest)

def rms_norm(values, gain_vec):
    return values * lax.rsqrt(lax.optimization_barrier(jnp.mean(values * values, axis=-1, keepdims=True)) + epsilon) * gain_vec

def gelu_tanh(values):
    return 0.5 * values * (1.0 + jnp.tanh(gelu_scale * (values + 0.044715 * values * values * values)))

def sigmoid(values):
    return 1.0 / (1.0 + jnp.exp(-values))

def soft_weights(scores):
    largest = lax.optimization_barrier(jnp.max(scores, axis=-1, keepdims=True))
    raised = jnp.exp(scores - largest)
    return raised / lax.optimization_barrier(jnp.sum(raised, axis=-1, keepdims=True))

def light_attention(normed, seg_row, weights_qkv, weights_out):
    length = normed.shape[0]
    inner_dim = weights_out.shape[0]
    activations = both_ways(product(normed, weights_qkv))
    query_heads = activations[:, :inner_dim].reshape(length, L_HEADS, L_HEAD)
    key_heads = activations[:, inner_dim:2 * inner_dim].reshape(length, L_HEADS, L_HEAD)
    value_heads = activations[:, 2 * inner_dim:].reshape(length, L_HEADS, L_HEAD)
    pad_spec = ((WINDOW, WINDOW), (0, 0), (0, 0))
    keys_padded = jnp.pad(key_heads, pad_spec)
    values_padded = jnp.pad(value_heads, pad_spec)
    seg_padded = jnp.pad(seg_row, (WINDOW, WINDOW), constant_values=-1)
    block_len = min(512, length)
    span_len = block_len + 2 * WINDOW
    offsets = jnp.arange(block_len)[:, None] - (jnp.arange(span_len)[None, :] - WINDOW)
    in_reach = jnp.abs(offsets) <= WINDOW

    def one_block(start):
        q_block = lax.dynamic_slice_in_dim(query_heads, start, block_len, 0)
        k_block = lax.dynamic_slice_in_dim(keys_padded, start, span_len, 0)
        v_block = lax.dynamic_slice_in_dim(values_padded, start, span_len, 0)
        q_seg = lax.dynamic_slice_in_dim(seg_row, start, block_len, 0)
        k_seg = lax.dynamic_slice_in_dim(seg_padded, start, span_len, 0)
        allowed = in_reach & (q_seg[:, None] == k_seg[None, :])
        scores = low_back(jnp.einsum('qhe,khe->hqk', q_block, k_block, precision=highest) * L_HEAD ** (-0.5))
        probs_soft = soft_weights(jnp.where(allowed[None], scores, masked_score))
        mixed_out = jnp.einsum('hqk,khe->qhe', low(probs_soft), v_block, precision=highest)
        return both_ways(mixed_out.reshape(block_len, inner_dim))
    starts = (jnp.arange(length // block_len) * block_len).astype(jnp.int32)
    mixed_all = lax.map(jax.checkpoint(one_block), starts).reshape(length, inner_dim)
    return low_back(product(mixed_all, weights_out))

def heavy_attention(normed, seg_row, slot_index, slot_count, weights_qkv, weights_out, router):
    routed_total = slot_index.shape[1]
    slot_ids = jnp.arange(routed_total)
    q_live = slot_ids < slot_count[0]
    kv_live = slot_ids < slot_count[1]
    q_mask = q_live[:, None].astype(normed.dtype)
    q_rows = low_back(normed[slot_index[0]] * q_mask)
    kv_rows = low_back(normed[slot_index[1]] * kv_live[:, None].astype(normed.dtype))
    inner_dim = weights_out.shape[0]
    head_q = both_ways(product(q_rows, weights_qkv[:, :inner_dim])).reshape(routed_total, H_HEADS, H_HEAD)
    kv_acts = both_ways(product(kv_rows, weights_qkv[:, inner_dim:]))
    head_k = kv_acts[:, :inner_dim].reshape(routed_total, H_HEADS, H_HEAD)
    head_v = kv_acts[:, inner_dim:].reshape(routed_total, H_HEADS, H_HEAD)
    allowed = (seg_row[slot_index[0]][:, None] == seg_row[slot_index[1]][None, :]) & kv_live[None, :]
    scores = low_back(jnp.einsum('qhe,khe->hqk', head_q, head_k, precision=highest) * H_HEAD ** (-0.5))
    probs_soft = soft_weights(jnp.where(allowed[None], scores, masked_score))
    mixed_out = low_back(jnp.einsum('hqk,khe->qhe', low(probs_soft), head_v, precision=highest).reshape(routed_total, inner_dim))
    gate_value = sigmoid(product(q_rows, router))
    gated = both_ways(gate_value[:, None] * mixed_out)
    rows_out = both_ways(product(gated, weights_out))
    return jnp.zeros_like(normed).at[slot_index[0]].add(rows_out * q_mask)

def light_feed(normed, gate_up, down_proj):
    hidden_width = down_proj.shape[0]
    pre_act = low_back(product(normed, gate_up))
    hidden_act = both_ways(gelu_tanh(pre_act[:, :hidden_width]) * pre_act[:, hidden_width:])
    return low_back(product(hidden_act, down_proj))

def heavy_feed(normed, slot_index, slot_count, gate_up, down_proj, router):
    live_mask = (jnp.arange(slot_index.shape[1]) < slot_count[2])[:, None].astype(normed.dtype)
    ffn_rows = low_back(normed[slot_index[2]] * live_mask)
    hidden_width = down_proj.shape[0]
    pre_act = low_back(product(ffn_rows, gate_up))
    gate_value = sigmoid(product(ffn_rows, router))
    hidden_act = both_ways(gate_value[:, None] * gelu_tanh(pre_act[:, :hidden_width]) * pre_act[:, hidden_width:])
    rows_out = both_ways(product(hidden_act, down_proj))
    return jnp.zeros_like(normed).at[slot_index[2]].add(rows_out * live_mask)

def layer(inputs, seg_row, slot_index, slot_count, weights):
    attn_gain, light_qkv, light_out, heavy_qkv, heavy_out, attn_router, ffn_gain, light_gate_up, light_down, heavy_gate_up, heavy_down, ffn_router = weights
    normed = low(rms_norm(inputs, attn_gain))
    midway = inputs + light_attention(normed, seg_row, light_qkv, light_out) + heavy_attention(normed, seg_row, slot_index, slot_count, heavy_qkv, heavy_out, attn_router)
    normed_ffn = low(rms_norm(midway, ffn_gain))
    return midway + light_feed(normed_ffn, light_gate_up, light_down) + heavy_feed(normed_ffn, slot_index, slot_count, heavy_gate_up, heavy_down, ffn_router)

def reference(layer_input, cotangent, segment_ids, route_index, route_count, attn_gain, light_qkv, light_out, heavy_qkv, heavy_out, attn_router, ffn_gain, light_gate_up, light_down, heavy_gate_up, heavy_down, ffn_router):
    weights = tuple((weight_arg.astype(jnp.float32) for weight_arg in (attn_gain, light_qkv, light_out, heavy_qkv, heavy_out, attn_router, ffn_gain, light_gate_up, light_down, heavy_gate_up, heavy_down, ffn_router)))

    def one_row(summed, row_parts):
        inputs, cot_row, seg_row, slot_index, slot_count = row_parts

        def run(values, params):
            return layer(values, seg_row, slot_index, slot_count, params)
        out_row, pull = jax.vjp(run, inputs.astype(jnp.float32), weights)
        row_input_grad, weight_grads = pull(cot_row.astype(jnp.float32))
        summed = tuple((acc_grad + new_grad for acc_grad, new_grad in zip(summed, weight_grads)))
        return (summed, (out_row.astype(jnp.bfloat16), row_input_grad.astype(jnp.bfloat16)))
    start_sums = tuple((jnp.zeros_like(weight_arg) for weight_arg in weights))
    totals, (outputs, input_grads) = lax.scan(one_row, start_sums, (layer_input, cotangent, segment_ids, route_index, route_count))
    return (outputs, input_grads, totals[0], totals[1], totals[2], totals[3], totals[4], totals[5], totals[6], totals[7], totals[8], totals[9], totals[10], totals[11])
```

```python
import jax
import jax.numpy as jnp
from jax import lax
from jax.experimental import pallas as pl
from jax.experimental.pallas import tpu as pltpu
from jax.sharding import PartitionSpec as P

L_HEADS = 8
L_HEAD = 96
H_HEADS = 12
H_HEAD = 64
WINDOW = 128
LANES = 128

epsilon = 1e-06
masked_score = -1e30
gelu_scale = 0.7978845608028654
bf16 = jnp.bfloat16
f32 = jnp.float32


def dma_moves(index, arrays, out_shapes, moves):
    def body(index_ref, *refs):
        ins, outs, sems = refs[: len(arrays)], refs[len(arrays) : -1], refs[-1]
        copies = [
            pltpu.make_async_copy(source(ins, index_ref), target(outs, index_ref), sems.at[k])
            for k, (source, target) in enumerate(moves)
        ]
        for copy in copies:
            copy.start()
        for copy in copies:
            copy.wait()

    return pl.pallas_call(
        body,
        out_shape=[jax.ShapeDtypeStruct(s, a) for s, a in out_shapes],
        in_specs=[pl.BlockSpec(memory_space=pltpu.SMEM)]
        + [pl.BlockSpec(memory_space=pl.ANY)] * len(arrays),
        out_specs=[pl.BlockSpec(memory_space=pltpu.VMEM)] * len(out_shapes),
        scratch_shapes=[pltpu.SemaphoreType.DMA((len(moves),))],
        compiler_params=pltpu.CompilerParams(vmem_limit_bytes=16 * 2**20),
    )(index, *arrays)


def dp_stages(count):
    if count == 8:
        return [
            lambda i: i ^ (2 + 2 * (i & 1)),
            lambda i: i ^ (4 - 2 * (i & 1)),
            lambda i: i ^ 1,
        ]
    masks = [1 << b for b in range(count.bit_length() - 1)][::-1]
    return [lambda i, m=m: i ^ m for m in masks]


def dp_sources(count):
    sources = [lambda i: i]
    for stage in dp_stages(count):
        sources = sources + [lambda i, f=f, stage=stage: f(stage(i)) for f in sources]
    return sources


def perm(count, stage):
    return [(i, stage(i)) for i in range(count)]


def seq_pieces(shard, count):
    return [shard] + [
        lax.ppermute(shard, "seq", [(i, i ^ k) for i in range(count)]) for k in range(1, count)
    ]


def gather_seq(shard):
    count, pos = lax.axis_size("seq"), lax.axis_index("seq")
    return place_seq(seq_pieces(shard, count), pos)


def place_seq(pieces, pos):
    count = len(pieces)
    order = jnp.stack([pos ^ k for k in range(count)]).astype(jnp.int32)
    moves = [
        (lambda ins, idx, k=k: ins[k], lambda outs, idx, k=k: outs[0].at[idx[k]])
        for k in range(count)
    ]
    shape = (count,) + pieces[0].shape
    return dma_moves(order, pieces, [(shape, pieces[0].dtype)], moves)[0]


def gather_dp(block, parts):
    count, me = lax.axis_size("dp"), lax.axis_index("dp")
    pieces = [block]
    for stage in dp_stages(count):
        pairs = perm(count, stage)
        pieces = pieces + [lax.ppermute(p, "dp", pairs) for p in pieces]
    order = jnp.stack([f(me) for f in dp_sources(count)]).astype(jnp.int32)
    moves, shapes = [], []
    for j, (shape, view) in enumerate(parts):
        shapes.append(((count,) + shape, block.dtype))
        for k in range(count):
            moves.append(
                (
                    lambda ins, idx, k=k, view=view: view(ins[k]),
                    lambda outs, idx, k=k, j=j: outs[j].at[idx[k]],
                )
            )
    return dma_moves(order, pieces, shapes, moves)


def scatter_dp(blocks):
    count, me = lax.axis_size("dp"), lax.axis_index("dp")
    order = jnp.stack([f(me) for f in dp_sources(count)]).astype(jnp.int32)
    half = count // 2
    shape = (half,) + blocks.shape[1:]
    moves = [
        (
            lambda ins, idx, k=k: ins[0].at[idx[k]],
            lambda outs, idx, k=k: outs[k // half].at[k % half],
        )
        for k in range(count)
    ]
    keep, send = dma_moves(order, [blocks], [(shape, bf16), (shape, bf16)], moves)
    for stage in dp_stages(count)[::-1]:
        got = lax.ppermute(send, "dp", perm(count, stage))
        total = keep.astype(f32) + got.astype(f32)
        half = half // 2
        if half:
            keep, send = total[:half].astype(bf16), total[half:].astype(bf16)
    return total[0]


def scatter_seq(blocks):
    count, pos = lax.axis_size("seq"), lax.axis_index("seq")
    sent = blocks.astype(bf16)
    total = lax.dynamic_index_in_dim(blocks, pos, 0, keepdims=False).astype(f32)
    for k in range(1, count):
        piece = lax.dynamic_index_in_dim(sent, pos ^ k, 0, keepdims=False)
        total = total + lax.ppermute(piece, "seq", [(i, i ^ k) for i in range(count)]).astype(f32)
    return total


def scatter_both(grad):
    dp, seq = lax.axis_size("dp"), lax.axis_size("seq")
    rows, columns = grad.shape
    blocks = grad.astype(bf16).reshape(dp, rows // dp, columns)
    mine = scatter_dp(blocks)
    return scatter_seq(mine.reshape(seq, rows // dp // seq, columns))


def sum_seq(part):
    count, mask = lax.axis_size("seq"), 1
    while mask < count:
        got = lax.ppermute(part, "seq", [(i, i ^ mask) for i in range(count)])
        part = (part.astype(f32) + got.astype(f32)).astype(bf16)
        mask *= 2
    return part


def after(value, *others):
    return lax.optimization_barrier((value,) + others)[0]


def inv_rms(values):
    return lax.rsqrt(jnp.mean(values * values, axis=-1, keepdims=True) + epsilon)


def norm_back(values, inv, scaled):
    inner = jnp.mean(scaled * values, axis=-1, keepdims=True)
    return inv * scaled - values * (inv * inv * inv) * inner


def gelu_both(v):
    inner = jnp.tanh(gelu_scale * (v + 0.044715 * v * v * v))
    value = 0.5 * v * (1.0 + inner)
    slope = 0.5 * (1.0 + inner) + 0.5 * v * (1.0 - inner * inner) * gelu_scale * (
        1.0 + 3.0 * 0.044715 * v * v
    )
    return value, slope


def sigmoid(values):
    return 1.0 / (1.0 + jnp.exp(-values))


def dot(a, b):
    return lax.dot_general(a, b, (((1,), (0,)), ((), ())), preferred_element_type=f32)


def dot_nt(a, b):
    return lax.dot_general(a, b, (((1,), (1,)), ((), ())), preferred_element_type=f32)


def dot_tn(a, b):
    return lax.dot_general(a, b, (((0,), (0,)), ((), ())), preferred_element_type=f32)


def route_table(slots, count, token_pos):
    live = jnp.arange(slots.shape[0]) < count
    return ((slots[:, None] == token_pos[None, :]) & live[:, None]).astype(bf16)


def heads(x, head):
    return x.reshape(x.shape[0], -1, head)


def attend(q, k, v, allowed, head):
    scores = jnp.einsum("qhe,khe->hqk", heads(q, head), heads(k, head), preferred_element_type=f32)
    scores = jnp.where(allowed[None], scores * head ** (-0.5), masked_score)
    largest = jnp.max(scores, axis=-1, keepdims=True)
    raised = jnp.exp(scores - largest)
    row_sum = jnp.sum(raised, axis=-1, keepdims=True)
    probs = (raised / row_sum).astype(bf16)
    mixed = jnp.einsum("hqk,khe->qhe", probs, heads(v, head), preferred_element_type=f32)
    return mixed.reshape(q.shape), largest + jnp.log(row_sum)


def attend_back(q, k, v, allowed, log_sum, grad, head):
    scale = head ** (-0.5)
    hq, hk, hv, hg = heads(q, head), heads(k, head), heads(v, head), heads(grad, head)
    scores = jnp.einsum("qhe,khe->hqk", hq, hk, preferred_element_type=f32) * scale
    probs = jnp.where(allowed[None], jnp.exp(scores - log_sum), 0.0)
    grad_probs = jnp.einsum("qhe,khe->hqk", hg, hv, preferred_element_type=f32)
    inner = jnp.sum(probs * grad_probs, axis=-1, keepdims=True)
    ds = (probs * (grad_probs - inner)).astype(bf16)
    grad_q = jnp.einsum("hqk,khe->qhe", ds, hk, preferred_element_type=f32) * scale
    grad_k = jnp.einsum("hqk,qhe->khe", ds, hq, preferred_element_type=f32) * scale
    grad_v = jnp.einsum("hqk,qhe->khe", probs.astype(bf16), hg, preferred_element_type=f32)
    grad_kv = jnp.concatenate([grad_k.reshape(k.shape), grad_v.reshape(k.shape)], axis=-1)
    return grad_q.reshape(q.shape).astype(bf16), grad_kv.astype(bf16)


def shards(
    layer_input,
    cotangent,
    segment_ids,
    route_index,
    route_count,
    attn_gain,
    light_qkv,
    light_out,
    heavy_qkv,
    heavy_out,
    attn_router,
    ffn_gain,
    light_gate_up,
    light_down,
    heavy_gate_up,
    heavy_down,
    ffn_router,
):
    dp, seq = lax.axis_size("dp"), lax.axis_size("seq")
    pos = lax.axis_index("seq")
    x_in, cot, seg = layer_input[0], cotangent[0], segment_ids[0]
    tokens, width = x_in.shape
    slots, counts = route_index[0], route_count[0]
    routed = slots.shape[1]
    token_pos = pos * tokens + jnp.arange(tokens, dtype=jnp.int32)
    table_q = route_table(slots[0], counts[0], token_pos)
    table_kv = route_table(slots[1], counts[1], token_pos)
    table_f = route_table(slots[2], counts[2], token_pos)

    marked = jnp.concatenate(
        [x_in, jnp.broadcast_to(seg.astype(bf16)[:, None], (tokens, LANES))], axis=1
    )
    left = lax.ppermute(marked[tokens - WINDOW :], "seq", [(i, i + 1) for i in range(seq - 1)])
    right = lax.ppermute(marked[:WINDOW], "seq", [(i + 1, i) for i in range(seq - 1)])
    kv_part = dot(table_kv, marked).astype(bf16)

    rows = light_qkv.shape[0]
    small = jnp.stack([attn_gain, attn_router, ffn_gain, ffn_router], axis=1)
    first = jnp.concatenate([light_qkv, jnp.pad(small, ((0, 0), (0, LANES - 4)))], axis=1)
    wide = light_qkv.shape[1]

    def full(parts):
        return [p.reshape(-1, p.shape[-1]) for p in parts]

    def whole_view(block):
        return [(block.shape, lambda r: r)]

    z_first = gather_seq(first)
    w_lqkv, small_all = full(
        gather_dp(
            z_first,
            [
                ((seq, rows, wide), lambda r: r.at[:, :, :wide]),
                ((seq, rows, LANES), lambda r: r.at[:, :, wide:]),
            ],
        )
    )
    kv_marked = sum_seq(kv_part)
    z_hqkv = gather_seq(after(heavy_qkv, z_first))
    (w_hqkv,) = full(gather_dp(z_hqkv, whole_view(z_hqkv)))
    z_outs = gather_seq(after(jnp.stack([light_out, heavy_out]), z_hqkv))
    w_lout, w_hout = full(
        gather_dp(
            z_outs,
            [((seq, rows, width), lambda r: r.at[:, 0]), ((seq, rows, width), lambda r: r.at[:, 1])],
        )
    )
    z_lgu = gather_seq(after(light_gate_up, z_outs))
    (w_lgu,) = full(gather_dp(z_lgu, whole_view(z_lgu)))
    z_down = gather_seq(after(light_down, z_lgu))
    (w_ldown,) = full(gather_dp(z_down, whole_view(z_down)))
    unit = heavy_down.shape[0]
    columns = heavy_gate_up.reshape(rows, 2 * dp, seq, unit)

    def hidden_columns(which):
        return lax.dynamic_index_in_dim(columns, which, 2, keepdims=False).reshape(rows, -1)

    own_columns = hidden_columns(pos)
    gu_pieces = [own_columns] + [
        lax.ppermute(
            after(hidden_columns(pos ^ k), z_lgu), "seq", [(i, i ^ k) for i in range(seq)]
        )
        for k in range(1, seq)
    ]
    z_hgu = place_seq(gu_pieces, pos)
    (w_hgu,) = full(gather_dp(z_hgu, whole_view(z_hgu)))
    (w_hdown,) = full(gather_dp(after(heavy_down, z_hgu), whole_view(heavy_down)))
    cot_rows = sum_seq(after(dot(table_f, cot).astype(bf16), z_outs))

    small_t = small_all[:, :4].T
    gain_attn = small_t[0].astype(f32)[None]
    router_attn = small_t[1][None]
    gain_ffn = small_t[2].astype(f32)[None]
    router_ffn = small_t[3][None]

    ext_marked = jnp.concatenate([left, marked, right], axis=0)
    ext_in = ext_marked[:, :width].astype(f32)
    ext_inv = inv_rms(ext_in)
    normed_ext = (ext_in * ext_inv * gain_attn).astype(bf16)
    normed = normed_ext[WINDOW : WINDOW + tokens]
    place = jnp.arange(tokens + 2 * WINDOW) - WINDOW
    outside = ((pos == 0) & (place < 0)) | ((pos == seq - 1) & (place >= tokens))
    key_seg = jnp.where(outside, -1.0, ext_marked[:, width].astype(f32))
    seg_f = seg.astype(f32)
    light_allowed = (jnp.abs(jnp.arange(tokens)[:, None] - place[None, :]) <= WINDOW) & (
        seg_f[:, None] == key_seg[None, :]
    )
    light_q = dot(normed, w_lqkv[:, :width]).astype(bf16)
    light_kv = dot(normed_ext, w_lqkv[:, width:]).astype(bf16)
    light_k, light_v = light_kv[:, :width], light_kv[:, width:]
    light_mixed, light_lse = attend(light_q, light_k, light_v, light_allowed, L_HEAD)
    light_mixed = light_mixed.astype(bf16)

    kv_in = kv_marked[:, :width].astype(f32)
    kv_inv = inv_rms(kv_in)
    kv_rows = (kv_in * kv_inv * gain_attn).astype(bf16)
    kv_seg = kv_marked[:, width].astype(f32)
    kv_live = jnp.arange(routed) < counts[1]
    q_rows = dot(table_q, normed).astype(bf16)
    q_seg = jnp.sum(table_q.astype(f32) * seg_f[None], axis=1)
    heavy_allowed = (q_seg[:, None] == kv_seg[None, :]) & kv_live[None, :]
    heavy_q = dot(q_rows, w_hqkv[:, :width]).astype(bf16)
    heavy_kv = dot(kv_rows, w_hqkv[:, width:]).astype(bf16)
    heavy_k, heavy_v = heavy_kv[:, :width], heavy_kv[:, width:]
    heavy_mixed, heavy_lse = attend(heavy_q, heavy_k, heavy_v, heavy_allowed, H_HEAD)
    gate = sigmoid(
        jnp.sum(q_rows.astype(f32) * router_attn.astype(f32), axis=1, keepdims=True)
    )
    gated = (gate * heavy_mixed).astype(bf16)
    heavy_rows = dot(gated, w_hout).astype(bf16)
    midway = x_in.astype(f32) + dot(light_mixed, w_lout) + dot_tn(table_q, heavy_rows)

    inv_ffn = inv_rms(midway)
    normed_ffn = (midway * inv_ffn * gain_ffn).astype(bf16)
    ffn_rows = sum_seq(dot(table_f, normed_ffn).astype(bf16))
    light_units = w_ldown.shape[0]
    light_pre = dot(normed_ffn, w_lgu)
    light_gate, light_up = light_pre[:, :light_units], light_pre[:, light_units:]
    light_act, light_slope = gelu_both(light_gate)
    light_hidden = (light_act * light_up).astype(bf16)
    light_ffn = dot(light_hidden, w_ldown)

    grad_light_down = dot_tn(light_hidden, cot)
    out_light_down = scatter_both(grad_light_down)
    hidden_grad = dot_nt(cot, w_ldown).astype(bf16).astype(f32)
    light_pre_grad = jnp.concatenate(
        [hidden_grad * light_up * light_slope, hidden_grad * light_act], axis=-1
    ).astype(bf16)
    out_light_gate_up = scatter_both(dot_tn(normed_ffn, light_pre_grad))
    normed_ffn_grad = dot_nt(light_pre_grad, w_lgu)

    heavy_units = w_hdown.shape[0]
    heavy_pre = dot(ffn_rows, w_hgu)
    heavy_gate, heavy_up = heavy_pre[:, :heavy_units], heavy_pre[:, heavy_units:]
    heavy_act, heavy_slope = gelu_both(heavy_gate)
    ffn_gate = sigmoid(
        jnp.sum(ffn_rows.astype(f32) * router_ffn.astype(f32), axis=1, keepdims=True)
    )
    heavy_hidden = (ffn_gate * heavy_act * heavy_up).astype(bf16)
    heavy_grad = dot_nt(cot_rows, w_hdown).astype(bf16).astype(f32)
    heavy_pre_grad = jnp.concatenate(
        [heavy_grad * ffn_gate * heavy_up * heavy_slope, heavy_grad * ffn_gate * heavy_act],
        axis=-1,
    ).astype(bf16)
    ffn_score_grad = (
        ffn_gate
        * (1.0 - ffn_gate)
        * jnp.sum(heavy_grad * heavy_act * heavy_up, axis=1, keepdims=True)
    )
    rows_grad_part = dot_nt(heavy_pre_grad, w_hgu) + ffn_score_grad * router_ffn.astype(f32)
    rows_grad = sum_seq(rows_grad_part.astype(bf16))
    heavy_out_rows = sum_seq(after(dot(heavy_hidden, w_hdown).astype(bf16), rows_grad))
    layer_output = (midway + light_ffn + dot_tn(table_f, heavy_out_rows)).astype(bf16)
    grad_ffn_router = jnp.sum(ffn_rows.astype(f32) * ffn_score_grad, axis=0)
    grad_hdown = dot_tn(heavy_hidden, cot_rows).astype(bf16)
    out_heavy_down = scatter_dp(grad_hdown.reshape(dp, unit, width))
    grad_hgu = dot_tn(ffn_rows, heavy_pre_grad).astype(bf16)
    hgu_mine = scatter_dp(grad_hgu.reshape(dp, width // dp, -1)).astype(bf16)
    hgu_mine = hgu_mine.reshape(seq, rows, -1)
    hgu_got = [lax.dynamic_index_in_dim(hgu_mine, pos, 0, keepdims=False)] + [
        lax.ppermute(
            lax.dynamic_index_in_dim(hgu_mine, pos ^ k, 0, keepdims=False),
            "seq",
            [(i, i ^ k) for i in range(seq)],
        )
        for k in range(1, seq)
    ]
    hgu_slices = place_seq(hgu_got, pos).reshape(seq, rows, 2 * dp, unit)
    out_heavy_gate_up = hgu_slices.transpose(1, 2, 0, 3).astype(f32).reshape(rows, -1)

    normed_ffn_grad = normed_ffn_grad + dot_tn(table_f, rows_grad)
    grad_ffn_gain = jnp.sum(normed_ffn_grad * midway * inv_ffn, axis=0)
    midway_grad = cot.astype(f32) + norm_back(midway, inv_ffn, normed_ffn_grad * gain_ffn)

    out_grad = midway_grad.astype(bf16)
    grad_lout = dot_tn(light_mixed, out_grad).astype(bf16)
    heavy_out_cot = dot(table_q, out_grad).astype(bf16)
    grad_hout = dot_tn(gated, heavy_out_cot).astype(bf16)
    outs_pair = jnp.stack(
        [grad_lout.reshape(dp, width // dp, width), grad_hout.reshape(dp, width // dp, width)],
        axis=1,
    )
    outs_mine = scatter_dp(outs_pair).reshape(2, seq, rows, width).transpose(1, 0, 2, 3)
    out_outs = scatter_seq(outs_mine)
    mixed_grad = dot_nt(out_grad, w_lout).astype(bf16)
    light_q_grad, light_kv_grad = attend_back(
        light_q, light_k, light_v, light_allowed, light_lse, mixed_grad, L_HEAD
    )
    grad_lqkv = jnp.concatenate(
        [dot_tn(normed, light_q_grad), dot_tn(normed_ext, light_kv_grad)], axis=1
    )
    out_light_qkv = scatter_both(grad_lqkv)
    ext_grad = dot_nt(light_kv_grad, w_lqkv[:, width:])

    gated_grad = dot_nt(heavy_out_cot, w_hout).astype(bf16).astype(f32)
    heavy_mixed_grad = (gate * gated_grad).astype(bf16)
    attn_score_grad = gate * (1.0 - gate) * jnp.sum(gated_grad * heavy_mixed, axis=1, keepdims=True)
    heavy_q_grad, heavy_kv_grad = attend_back(
        heavy_q, heavy_k, heavy_v, heavy_allowed, heavy_lse, heavy_mixed_grad, H_HEAD
    )
    grad_attn_router = jnp.sum(q_rows.astype(f32) * attn_score_grad, axis=0)
    q_rows_grad = (
        dot_nt(heavy_q_grad, w_hqkv[:, :width]) + attn_score_grad * router_attn.astype(f32)
    ).astype(bf16)
    kv_rows_grad = dot_nt(heavy_kv_grad, w_hqkv[:, width:])

    own_grad = (
        ext_grad[WINDOW : WINDOW + tokens]
        + dot_nt(light_q_grad, w_lqkv[:, :width])
        + dot_tn(table_q, q_rows_grad)
    )
    grad_attn_gain = (
        jnp.sum(own_grad * (ext_in * ext_inv)[WINDOW : WINDOW + tokens], axis=0)
        + jnp.sum(ext_grad[:WINDOW] * (ext_in * ext_inv)[:WINDOW], axis=0)
        + jnp.sum(ext_grad[WINDOW + tokens :] * (ext_in * ext_inv)[WINDOW + tokens :], axis=0)
        + jnp.sum(kv_rows_grad * (kv_in * kv_inv), axis=0)
    )
    small_grads = jnp.stack([grad_attn_gain, grad_attn_router, grad_ffn_gain, grad_ffn_router], 1)
    grad_hqkv = jnp.concatenate(
        [
            dot_tn(q_rows, heavy_q_grad),
            dot_tn(kv_rows, heavy_kv_grad),
            jnp.pad(small_grads, ((0, 0), (0, LANES - 4))),
        ],
        axis=1,
    )
    out_hqkv_small = scatter_both(grad_hqkv)
    out_small = out_hqkv_small[:, wide : wide + 4].T

    kv_total = sum_seq(kv_rows_grad.astype(bf16))
    from_right = lax.ppermute(
        ext_grad[WINDOW + tokens :].astype(bf16), "seq", [(i, i + 1) for i in range(seq - 1)]
    )
    from_left = lax.ppermute(
        ext_grad[:WINDOW].astype(bf16), "seq", [(i + 1, i) for i in range(seq - 1)]
    )
    edge = jnp.concatenate(
        [from_right.astype(f32), jnp.zeros((tokens - 2 * WINDOW, width), f32), from_left.astype(f32)]
    )
    total_grad = own_grad + edge + dot_tn(table_kv, kv_total)
    x_wide = x_in.astype(f32)
    input_grad = midway_grad + norm_back(
        x_wide, ext_inv[WINDOW : WINDOW + tokens], total_grad * gain_attn
    )

    return (
        layer_output[None],
        input_grad.astype(bf16)[None],
        out_small[0],
        out_light_qkv,
        out_outs[0],
        out_hqkv_small[:, :wide],
        out_outs[1],
        out_small[1],
        out_small[2],
        out_light_gate_up,
        out_light_down,
        out_heavy_gate_up,
        out_heavy_down,
        out_small[3],
    )


def solution(mesh):
    both = ("dp", "seq")
    vector, matrix, tokens = P(both), P(both, None), P("dp", "seq", None)
    return jax.shard_map(
        shards,
        mesh=mesh,
        in_specs=(
            tokens,
            tokens,
            P("dp", "seq"),
            P("dp", None, None),
            P("dp", None),
            vector,
            matrix,
            matrix,
            matrix,
            matrix,
            vector,
            vector,
            matrix,
            matrix,
            matrix,
            matrix,
            vector,
        ),
        out_specs=(
            tokens,
            tokens,
            vector,
            matrix,
            matrix,
            matrix,
            matrix,
            vector,
            vector,
            matrix,
            matrix,
            matrix,
            matrix,
            vector,
        ),
        check_vma=False,
    )
```

```python
import jax
import jax.numpy as jnp
from jax import lax
from jax.experimental import pallas as pl
from jax.experimental.pallas import tpu as pltpu
from jax.sharding import PartitionSpec as P

L_HEADS = 8
L_HEAD = 96
H_HEADS = 12
H_HEAD = 64
WINDOW = 128
LANES = 128

epsilon = 1e-06
masked_score = -1e30
gelu_scale = 0.7978845608028654
bf16 = jnp.bfloat16
f32 = jnp.float32


def dma_moves(index, arrays, out_shapes, moves):
    def body(index_ref, *refs):
        ins, outs, sems = refs[: len(arrays)], refs[len(arrays) : -1], refs[-1]
        copies = [
            pltpu.make_async_copy(source(ins, index_ref), target(outs, index_ref), sems.at[k])
            for k, (source, target) in enumerate(moves)
        ]
        for copy in copies:
            copy.start()
        for copy in copies:
            copy.wait()

    return pl.pallas_call(
        body,
        out_shape=[jax.ShapeDtypeStruct(s, a) for s, a in out_shapes],
        in_specs=[pl.BlockSpec(memory_space=pltpu.SMEM)]
        + [pl.BlockSpec(memory_space=pl.ANY)] * len(arrays),
        out_specs=[pl.BlockSpec(memory_space=pltpu.VMEM)] * len(out_shapes),
        scratch_shapes=[pltpu.SemaphoreType.DMA((len(moves),))],
        compiler_params=pltpu.CompilerParams(vmem_limit_bytes=16 * 2**20),
    )(index, *arrays)


def dp_stages(count):
    if count == 8:
        return [
            lambda i: i ^ (2 + 2 * (i & 1)),
            lambda i: i ^ (4 - 2 * (i & 1)),
            lambda i: i ^ 1,
        ]
    masks = [1 << b for b in range(count.bit_length() - 1)][::-1]
    return [lambda i, m=m: i ^ m for m in masks]


def dp_labels(count):
    labels = [()]
    for stage in range(len(dp_stages(count))):
        labels = labels + [label + (stage,) for label in labels]
    return labels


def dp_order():
    count, me = lax.axis_size("dp"), lax.axis_index("dp")
    stages = dp_stages(count)

    def source(label):
        at = me
        for stage in label[::-1]:
            at = stages[stage](at)
        return at

    return jnp.stack([source(label) for label in dp_labels(count)]).astype(jnp.int32)


def perm(count, stage):
    return [(i, stage(i)) for i in range(count)]


def perm_seq(count, k):
    return [(i, i ^ k) for i in range(count)]


def place_seq(pieces):
    count, pos = len(pieces), lax.axis_index("seq")
    order = jnp.stack([pos ^ k for k in range(count)]).astype(jnp.int32)
    moves = [
        (lambda ins, idx, k=k: ins[k], lambda outs, idx, k=k: outs[0].at[idx[k]])
        for k in range(count)
    ]
    shape = (count,) + pieces[0].shape
    return dma_moves(order, pieces, [(shape, pieces[0].dtype)], moves)[0]


def send_seq(piece_for):
    count = lax.axis_size("seq")
    return [lax.ppermute(piece_for(k), "seq", perm_seq(count, k)) for k in range(1, count)]


def wave(pieces, hops):
    count = lax.axis_size("dp")
    stages = dp_stages(count)
    for label in [p for p in pieces if len(p) == hops]:
        for stage in range(label[-1] + 1 if label else 0, len(stages)):
            pieces[label + (stage,)] = lax.ppermute(
                pieces[label], "dp", perm(count, stages[stage])
            )


def arrived(pieces, hops, last=None):
    final = len(dp_stages(lax.axis_size("dp"))) - 1
    return [p for p in pieces if len(p) == hops and (last or p[-1] != final)]


def fence(*values):
    return lax.optimization_barrier(values) if len(values) > 1 else values


def fence_pieces(groups, *values):
    flat = [pieces[label] for pieces, labels in groups for label in labels]
    out = fence(*values, *flat)
    rest = list(out[len(values) :])
    for pieces, labels in groups:
        for label in labels:
            pieces[label] = rest.pop(0)
    return out[: len(values)]


def place_dp(held, widths):
    pieces = [held[label] for label in dp_labels(lax.axis_size("dp"))]
    count = len(pieces)
    lead = pieces[0].shape[:-1]
    moves, shapes, low = [], [], 0
    for j, columns in enumerate(widths):
        shapes.append(((count,) + lead + (columns,), bf16))
        for k in range(count):
            moves.append(
                (
                    lambda ins, idx, k=k, low=low, columns=columns: ins[k].at[
                        ..., pl.ds(low, columns)
                    ],
                    lambda outs, idx, k=k, j=j: outs[j].at[idx[k]],
                )
            )
        low += columns
    return [p.reshape(-1, p.shape[-1]) for p in dma_moves(dp_order(), pieces, shapes, moves)]


def scatter_dp(grads):
    count = lax.axis_size("dp")
    half = count // 2
    rows = grads[0].shape[1]
    width = sum(g.shape[2] for g in grads)
    moves, low = [], 0
    for j, grad in enumerate(grads):
        columns = grad.shape[2]
        for k in range(count):
            moves.append(
                (
                    lambda ins, idx, k=k, j=j: ins[j].at[idx[k]],
                    lambda outs, idx, k=k, low=low, columns=columns: outs[k // half].at[
                        k % half, :, pl.ds(low, columns)
                    ],
                )
            )
        low += columns
    shape = (half, rows, width)
    keep, send = dma_moves(dp_order(), grads, [(shape, bf16), (shape, bf16)], moves)
    return Scatter(keep, send)


class Scatter:
    def __init__(self, keep, send):
        self.keep, self.left = keep, dp_stages(lax.axis_size("dp"))
        self.hop(send)

    def hop(self, send):
        count = lax.axis_size("dp")
        self.got = lax.ppermute(send, "dp", perm(count, self.left.pop()))

    def step(self):
        half = self.keep.shape[0] // 2
        wide = lambda part: part.astype(f32)
        send = (wide(self.keep[half:]) + wide(self.got[half:])).astype(bf16)
        self.keep = (wide(self.keep[:half]) + wide(self.got[:half])).astype(bf16)
        self.hop(send)

    def finish(self):
        while self.left:
            self.step()
        return self.keep[0].astype(f32) + self.got[0].astype(f32)


def fence_sums(sums, *values):
    out = fence(*values, *[s.got for s in sums])
    for s, got in zip(sums, out[len(values) :]):
        s.got = got
    return out[: len(values)]


def scatter_seq(blocks):
    count, pos = lax.axis_size("seq"), lax.axis_index("seq")
    sent = blocks.astype(bf16)
    total = lax.dynamic_index_in_dim(blocks, pos, 0, keepdims=False)
    for k in range(1, count):
        piece = lax.dynamic_index_in_dim(sent, pos ^ k, 0, keepdims=False)
        total = total + lax.ppermute(piece, "seq", perm_seq(count, k)).astype(f32)
    return total


def seq_masks():
    return [1 << b for b in range(lax.axis_size("seq").bit_length() - 1)]


def sum_hop(part, mask):
    got = lax.ppermute(part, "seq", perm_seq(lax.axis_size("seq"), mask))
    return (part.astype(f32) + got.astype(f32)).astype(bf16)


def sum_seq(part):
    for mask in seq_masks():
        part = sum_hop(part, mask)
    return part


def inv_rms(values):
    return lax.rsqrt(jnp.mean(values * values, axis=-1, keepdims=True) + epsilon)


def norm_back(values, inv, scaled):
    inner = jnp.mean(scaled * values, axis=-1, keepdims=True)
    return inv * scaled - values * (inv * inv * inv) * inner


def gelu_both(v):
    inner = jnp.tanh(gelu_scale * (v + 0.044715 * v * v * v))
    value = 0.5 * v * (1.0 + inner)
    slope = 0.5 * (1.0 + inner) + 0.5 * v * (1.0 - inner * inner) * gelu_scale * (
        1.0 + 3.0 * 0.044715 * v * v
    )
    return value, slope


def sigmoid(values):
    return 1.0 / (1.0 + jnp.exp(-values))


def dot(a, b):
    return lax.dot_general(a, b, (((1,), (0,)), ((), ())), preferred_element_type=f32)


def dot_nt(a, b):
    return lax.dot_general(a, b, (((1,), (1,)), ((), ())), preferred_element_type=f32)


def dot_tn(a, b):
    return lax.dot_general(a, b, (((0,), (0,)), ((), ())), preferred_element_type=f32)


def route_table(slots, count, token_pos):
    live = jnp.arange(slots.shape[0]) < count
    return ((slots[:, None] == token_pos[None, :]) & live[:, None]).astype(bf16)


def head_windows(width, head):
    found = []
    for low in range(0, width, head):
        first, last = low // LANES, (low + head - 1) // LANES
        found.append((first * LANES, (last + 1) * LANES, low - first * LANES))
    return found


def head_lanes(rows, low, high, offset, head):
    lane = lax.broadcasted_iota(jnp.int32, (rows, high - low), 1)
    return (lane >= offset) & (lane < offset + head)


def add_tiles(tiles, low, values):
    for t in range(values.shape[1] // LANES):
        part = values[:, t * LANES : (t + 1) * LANES]
        k = low // LANES + t
        tiles[k] = part if tiles[k] is None else tiles[k] + part


def attend(q, kv, q_seg, k_seg, head, block, reach, out_type):
    count, width = q.shape
    keys = kv.shape[0]
    span = block + 2 * reach if reach else keys
    windows = head_windows(width, head)
    scale = head ** (-0.5)

    def body(q_ref, kv_ref, q_seg_ref, k_seg_ref, out_ref, prob_ref):
        start = pl.multiple_of(pl.program_id(0) * block, block) if reach else 0
        rows = pl.ds(start, span)
        allowed = q_seg_ref[...] == k_seg_ref[:, rows]
        if reach:
            ahead = lax.broadcasted_iota(jnp.int32, (block, span), 1) - lax.broadcasted_iota(
                jnp.int32, (block, span), 0
            )
            allowed = allowed & (ahead >= 0) & (ahead <= 2 * reach)
        tiles = [None] * (width // LANES)
        for h, (low, high, offset) in enumerate(windows):
            mine = head_lanes(block, low, high, offset, head)
            q_head = jnp.where(mine, q_ref[:, low:high], 0)
            scores = dot_nt(q_head, kv_ref[rows, low:high]) * scale
            scores = jnp.where(allowed, scores, masked_score)
            raised = jnp.exp(scores - jnp.max(scores, axis=-1, keepdims=True))
            probs = (raised * (1.0 / jnp.sum(raised, axis=-1, keepdims=True))).astype(bf16)
            prob_ref[h] = probs
            mixed = dot(probs, kv_ref[rows, width + low : width + high])
            add_tiles(tiles, low, jnp.where(mine, mixed, 0.0))
        for t, tile in enumerate(tiles):
            out_ref[:, t * LANES : (t + 1) * LANES] = tile.astype(out_type)

    return pl.pallas_call(
        body,
        grid=(count // block,),
        in_specs=[
            pl.BlockSpec((block, width), lambda b: (b, 0)),
            pl.BlockSpec((keys, 2 * width), lambda b: (0, 0)),
            pl.BlockSpec((block, 1), lambda b: (b, 0)),
            pl.BlockSpec((1, keys), lambda b: (0, 0)),
        ],
        out_specs=[
            pl.BlockSpec((block, width), lambda b: (b, 0)),
            pl.BlockSpec((len(windows), block, span), lambda b: (0, b, 0)),
        ],
        out_shape=[
            jax.ShapeDtypeStruct((count, width), out_type),
            jax.ShapeDtypeStruct((len(windows), count, span), bf16),
        ],
        compiler_params=pltpu.CompilerParams(vmem_limit_bytes=32 * 2**20),
        cost_estimate=pl.CostEstimate(
            flops=4 * count * span * width,
            transcendentals=len(windows) * count * span,
            bytes_accessed=2 * (2 * count * width + 2 * keys * width + len(windows) * count * span),
        ),
    )(q, kv, q_seg[:, None], k_seg[None])


def attend_back(q, kv, probs, grad, head, block, reach):
    count, width = q.shape
    keys = kv.shape[0]
    span = block + 2 * reach if reach else keys
    windows = head_windows(width, head)
    scale = head ** (-0.5)

    def body(q_ref, kv_ref, prob_ref, grad_ref, q_grad_ref, kv_grad_ref, sums_ref):
        step = pl.program_id(0)

        @pl.when(step == 0)
        def _():
            sums_ref[...] = jnp.zeros_like(sums_ref)

        start = pl.multiple_of(step * block, block) if reach else 0
        rows = pl.ds(start, span)
        tiles = [None] * (width // LANES)
        for h, (low, high, offset) in enumerate(windows):
            mine = head_lanes(block, low, high, offset, head)
            q_head = jnp.where(mine, q_ref[:, low:high], 0)
            g_head = jnp.where(mine, grad_ref[:, low:high], 0)
            p_head = prob_ref[h]
            p_wide = p_head.astype(f32)
            p_grad = dot_nt(g_head, kv_ref[rows, width + low : width + high])
            inner = jnp.sum(p_wide * p_grad, axis=-1, keepdims=True)
            s_grad = (p_wide * (p_grad - inner)).astype(bf16)
            q_part = dot(s_grad, kv_ref[rows, low:high]) * scale
            add_tiles(tiles, low, jnp.where(mine, q_part, 0.0))
            sums_ref[rows, low:high] += dot_tn(s_grad, q_head) * scale
            sums_ref[rows, width + low : width + high] += dot_tn(p_head, g_head)
        for t, tile in enumerate(tiles):
            q_grad_ref[:, t * LANES : (t + 1) * LANES] = tile.astype(bf16)

        @pl.when(step == count // block - 1)
        def _():
            kv_grad_ref[...] = sums_ref[...].astype(bf16)

    return pl.pallas_call(
        body,
        grid=(count // block,),
        in_specs=[
            pl.BlockSpec((block, width), lambda b: (b, 0)),
            pl.BlockSpec((keys, 2 * width), lambda b: (0, 0)),
            pl.BlockSpec((len(windows), block, span), lambda b: (0, b, 0)),
            pl.BlockSpec((block, width), lambda b: (b, 0)),
        ],
        out_specs=[
            pl.BlockSpec((block, width), lambda b: (b, 0)),
            pl.BlockSpec((keys, 2 * width), lambda b: (0, 0)),
        ],
        out_shape=[
            jax.ShapeDtypeStruct((count, width), bf16),
            jax.ShapeDtypeStruct((keys, 2 * width), bf16),
        ],
        scratch_shapes=[pltpu.VMEM((keys, 2 * width), f32)],
        compiler_params=pltpu.CompilerParams(vmem_limit_bytes=40 * 2**20),
        cost_estimate=pl.CostEstimate(
            flops=8 * count * span * width,
            transcendentals=0,
            bytes_accessed=2 * (3 * count * width + 4 * keys * width + len(windows) * count * span),
        ),
    )(q, kv, probs, grad)


def shards(
    layer_input,
    cotangent,
    segment_ids,
    route_index,
    route_count,
    attn_gain,
    light_qkv,
    light_out,
    heavy_qkv,
    heavy_out,
    attn_router,
    ffn_gain,
    light_gate_up,
    light_down,
    heavy_gate_up,
    heavy_down,
    ffn_router,
):
    dp, seq = lax.axis_size("dp"), lax.axis_size("seq")
    pos = lax.axis_index("seq")
    x_in, cot, seg = layer_input[0], cotangent[0], segment_ids[0]
    tokens, width = x_in.shape
    slots, counts = route_index[0], route_count[0]
    routed = slots.shape[1]
    token_pos = pos * tokens + jnp.arange(tokens, dtype=jnp.int32)
    table_q = route_table(slots[0], counts[0], token_pos)
    table_kv = route_table(slots[1], counts[1], token_pos)
    table_f = route_table(slots[2], counts[2], token_pos)

    rows, wide = light_qkv.shape
    unit = heavy_down.shape[0]
    merged = lambda block: block.reshape(-1, block.shape[-1])
    hops = len(dp_stages(dp))

    small = jnp.stack([attn_gain, attn_router, ffn_gain, ffn_router], axis=1)
    first = jnp.concatenate([light_qkv, jnp.pad(small, ((0, 0), (0, LANES - 4)))], axis=1)
    got_first = send_seq(lambda k: first)
    marked = jnp.concatenate(
        [x_in, jnp.broadcast_to(seg.astype(bf16)[:, None], (tokens, LANES))], axis=1
    )
    left = lax.ppermute(marked[tokens - WINDOW :], "seq", [(i, i + 1) for i in range(seq - 1)])
    right = lax.ppermute(marked[:WINDOW], "seq", [(i + 1, i) for i in range(seq - 1)])
    kv_part = dot(table_kv, marked).astype(bf16)
    cot_part = dot(table_f, cot).astype(bf16)
    second = jnp.concatenate([heavy_qkv, light_out, heavy_out], axis=1)
    kv_part, cot_part, second, *got_first = fence(kv_part, cot_part, second, *got_first)

    first_held = {(): merged(place_seq([first] + got_first))}
    wave(first_held, 0)
    got_second = send_seq(lambda k: second)
    seq_left = seq_masks()
    kv_part = sum_hop(kv_part, seq_left.pop(0))
    for h in range(1, hops):
        fence_pieces([(first_held, arrived(first_held, h))])
        wave(first_held, h)
    w_lqkv, small_all = place_dp(first_held, [wide, LANES])

    small_t = small_all[:, :4].T
    gain_attn = small_t[0].astype(f32)[None]
    router_attn = small_t[1][None]
    gain_ffn = small_t[2].astype(f32)[None]
    router_ffn = small_t[3][None]

    ext_marked = jnp.concatenate([left, marked, right], axis=0)
    ext_in = ext_marked[:, :width].astype(f32)
    ext_inv = inv_rms(ext_in)
    normed_ext = (ext_in * ext_inv * gain_attn).astype(bf16)
    normed = normed_ext[WINDOW : WINDOW + tokens]
    place = jnp.arange(tokens + 2 * WINDOW) - WINDOW
    outside = ((pos == 0) & (place < 0)) | ((pos == seq - 1) & (place >= tokens))
    key_seg = jnp.where(outside, -1.0, ext_marked[:, width].astype(f32))
    seg_f = seg.astype(f32)
    light_q = dot(normed, w_lqkv[:, :width]).astype(bf16)
    light_kv = dot(normed_ext, w_lqkv[:, width:]).astype(bf16)
    z_second = merged(place_seq([second] + got_second))
    light_q, light_kv, kv_part, z_second = fence(light_q, light_kv, kv_part, z_second)
    second_held = {(): z_second}
    wave(second_held, 0)
    for mask in seq_left:
        kv_part = sum_hop(kv_part, mask)
    light_mixed, light_probs = attend(
        light_q, light_kv, seg_f, key_seg, L_HEAD, WINDOW, WINDOW, bf16
    )
    q_rows = dot(table_q, normed).astype(bf16)
    q_seg = jnp.sum(table_q.astype(f32) * seg_f[None], axis=1)
    columns = heavy_gate_up.reshape(rows, 2 * dp, seq, unit)
    light_mixed, q_rows, kv_marked, gate_up, columns, down = fence_pieces(
        [(second_held, arrived(second_held, 1))],
        light_mixed, q_rows, kv_part, light_gate_up, columns, light_down
    )

    for h in range(1, hops):
        wave(second_held, h)

    def gate_up_for(k):
        own = lax.dynamic_index_in_dim(columns, pos ^ k, 2, keepdims=False)
        return jnp.concatenate([gate_up, own.reshape(rows, -1)], axis=1)

    got_gate_up = send_seq(gate_up_for)
    got_down = send_seq(lambda k: down)
    w_hqkv, w_lout, w_hout = place_dp(second_held, [wide, width, width])

    kv_in = kv_marked[:, :width].astype(f32)
    kv_inv = inv_rms(kv_in)
    kv_rows = (kv_in * kv_inv * gain_attn).astype(bf16)
    kv_seg = jnp.where(jnp.arange(routed) < counts[1], kv_marked[:, width].astype(f32), -1.0)
    heavy_q = dot(q_rows, w_hqkv[:, :width]).astype(bf16)
    heavy_kv = dot(kv_rows, w_hqkv[:, width:]).astype(bf16)
    heavy_mixed, heavy_probs = attend(
        heavy_q, heavy_kv, q_seg, kv_seg, H_HEAD, min(routed, 256), 0, f32
    )
    gate = sigmoid(
        jnp.sum(q_rows.astype(f32) * router_attn.astype(f32), axis=1, keepdims=True)
    )
    gated = (gate * heavy_mixed).astype(bf16)
    heavy_rows = dot(gated, w_hout).astype(bf16)
    midway = x_in.astype(f32) + dot(light_mixed, w_lout) + dot_tn(table_q, heavy_rows)

    inv_ffn = inv_rms(midway)
    normed_ffn = (midway * inv_ffn * gain_ffn).astype(bf16)
    rows_part = dot(table_f, normed_ffn).astype(bf16)
    rows_part, normed_ffn, cot_part, *got = fence(
        rows_part, normed_ffn, cot_part, *got_gate_up, *got_down
    )
    got_gate_up, got_down = got[: seq - 1], got[seq - 1 :]
    gate_up_held = {(): merged(place_seq([gate_up_for(0)] + got_gate_up))}
    z_down = merged(place_seq([down] + got_down))
    if z_down.shape == heavy_down.shape:
        down_held = [{(): jnp.concatenate([z_down, heavy_down], axis=1)}]
    else:
        down_held = [{(): z_down}, {(): heavy_down}]
    ffn_held = [gate_up_held] + down_held
    for held in ffn_held:
        wave(held, 0)
    seq_left = seq_masks()
    rows_part = sum_hop(rows_part, seq_left.pop(0))
    rows_part, normed_ffn, cot_part = fence_pieces(
        [(held, arrived(held, 1)) for held in ffn_held], rows_part, normed_ffn, cot_part
    )
    for h in range(1, hops):
        for held in ffn_held:
            wave(held, h)
    for mask in seq_left:
        rows_part = sum_hop(rows_part, mask)
    w_lgu, w_hgu = place_dp(gate_up_held, [light_gate_up.shape[1], 2 * dp * unit])
    w_ldown, w_hdown = sum(
        [place_dp(held, [width] * (2 // len(down_held))) for held in down_held], []
    )
    ffn_rows, cot_part, normed_ffn = fence(rows_part, cot_part, normed_ffn)
    cot_rows = sum_seq(cot_part)

    by_dp = lambda grad: grad.reshape(dp, -1, grad.shape[1])
    light_units = w_ldown.shape[0]
    light_pre = dot(normed_ffn, w_lgu)
    light_gate, light_up = light_pre[:, :light_units], light_pre[:, light_units:]
    light_act, light_slope = gelu_both(light_gate)
    light_hidden = (light_act * light_up).astype(bf16)
    light_ffn = dot(light_hidden, w_ldown)
    grad_ldown = dot_tn(light_hidden, cot).astype(bf16)
    hidden_grad = dot_nt(cot, w_ldown).astype(bf16).astype(f32)
    light_pre_grad = jnp.concatenate(
        [hidden_grad * light_up * light_slope, hidden_grad * light_act], axis=-1
    ).astype(bf16)
    grad_lgu = dot_tn(normed_ffn, light_pre_grad).astype(bf16)
    normed_ffn_grad = dot_nt(light_pre_grad, w_lgu)
    ffn_rows, cot_rows, normed_ffn_grad, grad_ldown, grad_lgu = fence(
        ffn_rows, cot_rows, normed_ffn_grad, grad_ldown, grad_lgu
    )

    sum_light = [scatter_dp([by_dp(grad_lgu)]), scatter_dp([by_dp(grad_ldown)])]
    heavy_units = w_hdown.shape[0]
    heavy_pre = dot(ffn_rows, w_hgu)
    heavy_gate, heavy_up = heavy_pre[:, :heavy_units], heavy_pre[:, heavy_units:]
    heavy_act, heavy_slope = gelu_both(heavy_gate)
    ffn_gate = sigmoid(
        jnp.sum(ffn_rows.astype(f32) * router_ffn.astype(f32), axis=1, keepdims=True)
    )
    heavy_hidden = (ffn_gate * heavy_act * heavy_up).astype(bf16)
    heavy_grad = dot_nt(cot_rows, w_hdown).astype(bf16).astype(f32)
    heavy_pre_grad = jnp.concatenate(
        [heavy_grad * ffn_gate * heavy_up * heavy_slope, heavy_grad * ffn_gate * heavy_act],
        axis=-1,
    ).astype(bf16)
    ffn_score_grad = (
        ffn_gate
        * (1.0 - ffn_gate)
        * jnp.sum(heavy_grad * heavy_act * heavy_up, axis=1, keepdims=True)
    )
    rows_grad_part = dot_nt(heavy_pre_grad, w_hgu) + ffn_score_grad * router_ffn.astype(f32)
    rows_grad = rows_grad_part.astype(bf16)
    rows_grad, heavy_hidden, heavy_pre_grad, ffn_score_grad = fence_sums(
        sum_light, rows_grad, heavy_hidden, heavy_pre_grad, ffn_score_grad
    )
    seq_left = seq_masks()
    rows_grad = sum_hop(rows_grad, seq_left.pop(0))
    for s in sum_light:
        s.step()
    grad_ffn_router = jnp.sum(ffn_rows.astype(f32) * ffn_score_grad, axis=0)
    grad_hdown = dot_tn(heavy_hidden, cot_rows).astype(bf16)
    grad_hgu = dot_tn(ffn_rows, heavy_pre_grad).astype(bf16)
    out_part = dot(heavy_hidden, w_hdown).astype(bf16)
    rows_grad, grad_hdown, grad_hgu, out_part = fence_sums(
        sum_light, rows_grad, grad_hdown, grad_hgu, out_part
    )
    for mask in seq_left:
        rows_grad = sum_hop(rows_grad, mask)
    for s in sum_light:
        s.step()
    sum_heavy = [scatter_dp([by_dp(grad_hgu)]), scatter_dp([by_dp(grad_hdown)])]
    rows_grad, out_part = fence_sums(sum_light + sum_heavy, rows_grad, out_part)

    for s in sum_heavy:
        s.step()
    out_left = seq_masks()
    out_part = sum_hop(out_part, out_left.pop(0))
    lgu_mine = sum_light[0].finish().reshape(seq, rows, -1)
    ldown_mine = sum_light[1].finish().reshape(seq, -1, width)
    normed_ffn_grad = normed_ffn_grad + dot_tn(table_f, rows_grad)
    grad_ffn_gain = jnp.sum(normed_ffn_grad * midway * inv_ffn, axis=0)
    midway_grad = cot.astype(f32) + norm_back(midway, inv_ffn, normed_ffn_grad * gain_ffn)

    out_grad = midway_grad.astype(bf16)
    grad_lout = dot_tn(light_mixed, out_grad).astype(bf16)
    heavy_out_cot = dot(table_q, out_grad).astype(bf16)
    grad_hout = dot_tn(gated, heavy_out_cot).astype(bf16)
    gated_grad = dot_nt(heavy_out_cot, w_hout).astype(bf16).astype(f32)
    heavy_mixed_grad = (gate * gated_grad).astype(bf16)
    attn_score_grad = gate * (1.0 - gate) * jnp.sum(gated_grad * heavy_mixed, axis=1, keepdims=True)
    heavy_q_grad, heavy_kv_grad = attend_back(
        heavy_q, heavy_kv, heavy_probs, heavy_mixed_grad, H_HEAD, min(routed, 256), 0
    )
    grad_hq = dot_tn(q_rows, heavy_q_grad).astype(bf16)
    grad_hkv = dot_tn(kv_rows, heavy_kv_grad).astype(bf16)
    grad_attn_router = jnp.sum(q_rows.astype(f32) * attn_score_grad, axis=0)
    q_rows_grad = (
        dot_nt(heavy_q_grad, w_hqkv[:, :width]) + attn_score_grad * router_attn.astype(f32)
    ).astype(bf16)
    kv_rows_grad = dot_nt(heavy_kv_grad, w_hqkv[:, width:])
    mixed_grad = dot_nt(out_grad, w_lout).astype(bf16)
    mixed_grad, kv_send, out_part, lgu_mine, ldown_mine, *attn_grads = fence_sums(
        sum_heavy,
        mixed_grad,
        kv_rows_grad.astype(bf16),
        out_part,
        lgu_mine,
        ldown_mine,
        *[by_dp(g) for g in (grad_hq, grad_hkv, grad_lout, grad_hout)],
    )

    for s in sum_heavy:
        s.step()
    sum_attn = scatter_dp(attn_grads)
    for mask in out_left:
        out_part = sum_hop(out_part, mask)
    kv_left = seq_masks()
    kv_send = sum_hop(kv_send, kv_left.pop(0))
    light_q_grad, light_kv_grad = attend_back(
        light_q, light_kv, light_probs, mixed_grad, L_HEAD, WINDOW, WINDOW
    )
    light_q_grad, light_kv_grad, kv_send, out_part, lgu_mine, ldown_mine = fence_sums(
        sum_heavy + [sum_attn], light_q_grad, light_kv_grad, kv_send, out_part, lgu_mine, ldown_mine
    )
    sum_attn.step()
    for mask in kv_left:
        kv_send = sum_hop(kv_send, mask)
    out_light_down = scatter_seq(ldown_mine)
    hgu_mine = sum_heavy[0].finish().reshape(seq, rows, -1)
    out_heavy_down = sum_heavy[1].finish()
    ext_grad = dot_nt(light_kv_grad, w_lqkv[:, width:])

    own_grad = (
        ext_grad[WINDOW : WINDOW + tokens]
        + dot_nt(light_q_grad, w_lqkv[:, :width])
        + dot_tn(table_q, q_rows_grad)
    )
    grad_attn_gain = (
        jnp.sum(own_grad * (ext_in * ext_inv)[WINDOW : WINDOW + tokens], axis=0)
        + jnp.sum(ext_grad[:WINDOW] * (ext_in * ext_inv)[:WINDOW], axis=0)
        + jnp.sum(ext_grad[WINDOW + tokens :] * (ext_in * ext_inv)[WINDOW + tokens :], axis=0)
        + jnp.sum(kv_rows_grad * (kv_in * kv_inv), axis=0)
    )
    small_grads = jnp.stack([grad_attn_gain, grad_attn_router, grad_ffn_gain, grad_ffn_router], 1)
    grad_lqkv = [
        dot_tn(normed, light_q_grad).astype(bf16),
        dot_tn(normed_ext, light_kv_grad).astype(bf16),
        jnp.pad(small_grads, ((0, 0), (0, LANES - 4))).astype(bf16),
    ]
    *grad_lqkv, hgu_mine, lgu_mine, out_light_down = fence_sums(
        [sum_attn], *[by_dp(g) for g in grad_lqkv], hgu_mine, lgu_mine, out_light_down
    )
    sum_last = scatter_dp(grad_lqkv)
    both = jnp.concatenate([lgu_mine.astype(bf16), hgu_mine.astype(bf16)], axis=2)
    pick = lambda k: lax.dynamic_index_in_dim(both, pos ^ k, 0, keepdims=False)
    got = [pick(0)] + send_seq(pick)
    from_right = lax.ppermute(
        ext_grad[WINDOW + tokens :].astype(bf16), "seq", [(i, i + 1) for i in range(seq - 1)]
    )
    from_left = lax.ppermute(
        ext_grad[:WINDOW].astype(bf16), "seq", [(i + 1, i) for i in range(seq - 1)]
    )
    sum_last.step()
    attn_mine = sum_attn.finish().reshape(seq, rows, -1)
    attn_mine, kv_total, *got = fence_sums([sum_last], attn_mine, kv_send, *got)
    sum_last.step()
    heavy_outs = scatter_seq(attn_mine)
    light_cut = light_gate_up.shape[1]
    out_light_gate_up = sum(g[:, :light_cut].astype(f32) for g in got)
    slices = place_seq(got)[:, :, light_cut:].reshape(seq, rows, 2 * dp, unit)
    out_heavy_gate_up = slices.transpose(1, 2, 0, 3).astype(f32).reshape(rows, -1)
    layer_output = (midway + light_ffn + dot_tn(table_f, out_part)).astype(bf16)
    light_outs = scatter_seq(sum_last.finish().reshape(seq, rows, -1))
    out_small = light_outs[:, wide : wide + 4].T
    edge = jnp.concatenate(
        [from_right.astype(f32), jnp.zeros((tokens - 2 * WINDOW, width), f32), from_left.astype(f32)]
    )
    total_grad = own_grad + edge + dot_tn(table_kv, kv_total)
    x_wide = x_in.astype(f32)
    input_grad = midway_grad + norm_back(
        x_wide, ext_inv[WINDOW : WINDOW + tokens], total_grad * gain_attn
    )

    return (
        layer_output[None],
        input_grad.astype(bf16)[None],
        out_small[0],
        light_outs[:, :wide],
        heavy_outs[:, wide : wide + width],
        heavy_outs[:, :wide],
        heavy_outs[:, wide + width :],
        out_small[1],
        out_small[2],
        out_light_gate_up,
        out_light_down,
        out_heavy_gate_up,
        out_heavy_down,
        out_small[3],
    )


def solution(mesh):
    both = ("dp", "seq")
    vector, matrix, tokens = P(both), P(both, None), P("dp", "seq", None)
    return jax.shard_map(
        shards,
        mesh=mesh,
        in_specs=(
            tokens,
            tokens,
            P("dp", "seq"),
            P("dp", None, None),
            P("dp", None),
            vector,
            matrix,
            matrix,
            matrix,
            matrix,
            vector,
            vector,
            matrix,
            matrix,
            matrix,
            matrix,
            vector,
        ),
        out_specs=(
            tokens,
            tokens,
            vector,
            matrix,
            matrix,
            matrix,
            matrix,
            vector,
            vector,
            matrix,
            matrix,
            matrix,
            matrix,
            vector,
        ),
        check_vma=False,
    )
```

```python
import jax
import jax.numpy as jnp
from jax import lax
from jax.experimental import pallas as pl
from jax.experimental.pallas import tpu as pltpu
from jax.sharding import PartitionSpec as P

L_HEADS = 8
L_HEAD = 96
H_HEADS = 12
H_HEAD = 64
WINDOW = 128
LANES = 128

epsilon = 1e-06
masked_score = -1e30
gelu_scale = 0.7978845608028654
bf16 = jnp.bfloat16
f32 = jnp.float32


def dma_moves(index, arrays, out_shapes, moves):
    def body(index_ref, *refs):
        ins, outs, sems = refs[: len(arrays)], refs[len(arrays) : -1], refs[-1]
        copies = [
            pltpu.make_async_copy(source(ins, index_ref), target(outs, index_ref), sems.at[k])
            for k, (source, target) in enumerate(moves)
        ]
        for copy in copies:
            copy.start()
        for copy in copies:
            copy.wait()

    return pl.pallas_call(
        body,
        out_shape=[jax.ShapeDtypeStruct(s, a) for s, a in out_shapes],
        in_specs=[pl.BlockSpec(memory_space=pltpu.SMEM)]
        + [pl.BlockSpec(memory_space=pl.ANY)] * len(arrays),
        out_specs=[pl.BlockSpec(memory_space=pltpu.VMEM)] * len(out_shapes),
        scratch_shapes=[pltpu.SemaphoreType.DMA((len(moves),))],
        compiler_params=pltpu.CompilerParams(vmem_limit_bytes=16 * 2**20),
    )(index, *arrays)


def dp_stages(count):
    if count == 8:
        return [
            lambda i: i ^ (2 + 2 * (i & 1)),
            lambda i: i ^ (4 - 2 * (i & 1)),
            lambda i: i ^ 1,
        ]
    masks = [1 << b for b in range(count.bit_length() - 1)][::-1]
    return [lambda i, m=m: i ^ m for m in masks]


def dp_labels(count):
    labels = [()]
    for stage in range(len(dp_stages(count))):
        labels = labels + [label + (stage,) for label in labels]
    return labels


def dp_order():
    count, me = lax.axis_size("dp"), lax.axis_index("dp")
    stages = dp_stages(count)

    def source(label):
        at = me
        for stage in label[::-1]:
            at = stages[stage](at)
        return at

    return jnp.stack([source(label) for label in dp_labels(count)]).astype(jnp.int32)


def perm(count, stage):
    return [(i, stage(i)) for i in range(count)]


def perm_seq(count, k):
    return [(i, i ^ k) for i in range(count)]


def fence(*values):
    return lax.optimization_barrier(values) if len(values) > 1 else values


def gate(value, *others):
    return lax.optimization_barrier((value,) + others)[0] if others else value


def seq_order(steps):
    pos = lax.axis_index("seq")
    return jnp.stack([pos ^ k for k in steps]).astype(jnp.int32)


def place_seq(pieces, widths=None):
    return place(pieces, seq_order(range(len(pieces))), widths or [pieces[0].shape[-1]])


def place(pieces, order, widths):
    count, lead = len(pieces), pieces[0].shape[:-1]
    moves, shapes, low = [], [], 0
    for j, columns in enumerate(widths):
        shapes.append(((count,) + lead + (columns,), bf16))
        for k in range(count):
            moves.append(
                (
                    lambda ins, idx, k=k, low=low, columns=columns: ins[k].at[
                        ..., pl.ds(low, columns)
                    ],
                    lambda outs, idx, k=k, j=j: outs[j].at[idx[k]],
                )
            )
        low += columns
    return [p.reshape(-1, p.shape[-1]) for p in dma_moves(order, pieces, shapes, moves)]


def fold(block, rows):
    count, width = block.shape[-2:]
    extra = count - rows
    if not extra:
        return block
    if rows % 8 or extra % 8 or extra < 0 or rows % extra or width % (rows // extra * LANES):
        return block.reshape(block.shape[:-2] + (rows, -1))
    groups = jnp.split(block[..., rows:, :], rows // extra, axis=-1)
    return jnp.concatenate([block[..., :rows, :], jnp.concatenate(groups, axis=-2)], axis=-1)


def unfold(block, count, width):
    rows = block.shape[-2]
    extra = count - rows
    if not extra:
        return block
    if rows % 8 or extra % 8 or extra < 0 or rows % extra or width % (rows // extra * LANES):
        return block.reshape(block.shape[:-2] + (count, width))
    groups = jnp.split(block[..., width:], rows // extra, axis=-2)
    return jnp.concatenate([block[..., :width], jnp.concatenate(groups, axis=-1)], axis=-2)


def send_seq(piece_for, every=1):
    count = lax.axis_size("seq")
    steps = range(every, count, every)
    return [lax.ppermute(piece_for(k), "seq", perm_seq(count, k)) for k in steps]


def wave(pieces, hops, *after):
    count = lax.axis_size("dp")
    stages = dp_stages(count)
    for label in [p for p in pieces if len(p) == hops]:
        later = range(label[-1] + 1 if label else 0, len(stages))
        if len(later):
            pieces[label] = gate(pieces[label], *after)
        for stage in later:
            pieces[label + (stage,)] = lax.ppermute(
                pieces[label], "dp", perm(count, stages[stage])
            )


def place_dp(held, widths, *after):
    pieces = [held[label] for label in dp_labels(lax.axis_size("dp"))]
    return place(pieces, gate(dp_order(), *after), widths)


def scatter_dp(grads):
    count = lax.axis_size("dp")
    half = count // 2
    rows = grads[0].shape[1]
    width = sum(g.shape[2] for g in grads)
    moves, low = [], 0
    for j, grad in enumerate(grads):
        columns = grad.shape[2]
        for k in range(count):
            moves.append(
                (
                    lambda ins, idx, k=k, j=j: ins[j].at[idx[k]],
                    lambda outs, idx, k=k, low=low, columns=columns: outs[k // half].at[
                        k % half, :, pl.ds(low, columns)
                    ],
                )
            )
        low += columns
    shape = (half, rows, width)
    keep, send = dma_moves(dp_order(), grads, [(shape, bf16), (shape, bf16)], moves)
    return Scatter(keep, send)


class Scatter:
    def __init__(self, keep, send):
        self.keep, self.left = keep, dp_stages(lax.axis_size("dp"))
        self.hop(send)

    def hop(self, send):
        count = lax.axis_size("dp")
        self.got = lax.ppermute(send, "dp", perm(count, self.left.pop()))

    def step(self, *after):
        self.keep = gate(self.keep, *after)
        half = self.keep.shape[0] // 2
        wide = lambda part: part.astype(f32)
        send = (wide(self.keep[half:]) + wide(self.got[half:])).astype(bf16)
        self.keep = (wide(self.keep[:half]) + wide(self.got[:half])).astype(bf16)
        self.hop(send)

    def finish(self, *after):
        while len(self.left):
            self.step(*after)
        return gate(self.keep, *after)[0].astype(f32) + self.got[0].astype(f32)


def pick_seq(blocks):
    pos = lax.axis_index("seq")
    return lambda k: lax.dynamic_index_in_dim(blocks, pos ^ k, 0, keepdims=False)


class Sum:
    def __init__(self, part, *after, pair=False):
        self.masks = [1 << b for b in range(lax.axis_size("seq").bit_length() - 1)]
        if pair:
            self.masks = self.masks[:1]
        self.part = gate(part, *after)
        self.send()

    def send(self):
        pairs = perm_seq(lax.axis_size("seq"), self.masks.pop(0))
        self.got = lax.ppermute(self.part, "seq", pairs)

    def add(self, *after):
        part = gate(self.part, *after)
        self.part = (part.astype(f32) + self.got.astype(f32)).astype(bf16)
        if self.masks:
            self.send()

    def finish(self, *after):
        while self.masks:
            self.add(*after)
        self.add(*after)
        return self.part


def split_columns(odd, weights, chunk):
    rows, width = weights.shape
    pairs = width // (2 * chunk)

    def body(odd_ref, weights_ref, own_ref, other_ref):
        def copy(own, other):
            for j in range(pairs):
                at = pl.ds(j * chunk, chunk)
                own[:, at] = weights_ref[:, pl.ds(2 * j * chunk, chunk)]
                other[:, at] = weights_ref[:, pl.ds((2 * j + 1) * chunk, chunk)]

        @pl.when(odd_ref[0] == 0)
        def _():
            copy(own_ref, other_ref)

        @pl.when(odd_ref[0] == 1)
        def _():
            copy(other_ref, own_ref)

    return pl.pallas_call(
        body,
        in_specs=[pl.BlockSpec(memory_space=pltpu.SMEM), pl.BlockSpec(memory_space=pltpu.VMEM)],
        out_specs=[pl.BlockSpec(memory_space=pltpu.VMEM)] * 2,
        out_shape=[jax.ShapeDtypeStruct((rows, width // 2), weights.dtype)] * 2,
    )(odd, weights)


def join_columns(odd, pieces, chunk):
    rows, width = pieces[0].shape
    count = len(pieces)

    def body(odd_ref, *refs):
        out_ref = refs[-1]

        def fill(first, second):
            for j in range(width // chunk):
                at = pl.ds(j * chunk, chunk)
                for side, group in enumerate((first, second)):
                    total = group[0][:, at].astype(f32)
                    for ref in group[1:]:
                        total = total + ref[:, at].astype(f32)
                    out_ref[:, pl.ds((2 * j + side) * chunk, chunk)] = total

        @pl.when(odd_ref[0] == 0)
        def _():
            fill(refs[0:count:2], refs[1:count:2])

        @pl.when(odd_ref[0] == 1)
        def _():
            fill(refs[1:count:2], refs[0:count:2])

    return pl.pallas_call(
        body,
        in_specs=[pl.BlockSpec(memory_space=pltpu.SMEM)]
        + [pl.BlockSpec(memory_space=pltpu.VMEM)] * count,
        out_specs=pl.BlockSpec(memory_space=pltpu.VMEM),
        out_shape=jax.ShapeDtypeStruct((rows, 2 * width), f32),
    )(odd, *pieces)


def inv_rms(values):
    return lax.rsqrt(jnp.mean(values * values, axis=-1, keepdims=True) + epsilon)


def norm_back(values, inv, scaled):
    inner = jnp.mean(scaled * values, axis=-1, keepdims=True)
    return inv * scaled - values * (inv * inv * inv) * inner


def gelu_both(v):
    inner = jnp.tanh(gelu_scale * (v + 0.044715 * v * v * v))
    value = 0.5 * v * (1.0 + inner)
    slope = 0.5 * (1.0 + inner) + 0.5 * v * (1.0 - inner * inner) * gelu_scale * (
        1.0 + 3.0 * 0.044715 * v * v
    )
    return value, slope


def sigmoid(values):
    return 1.0 / (1.0 + jnp.exp(-values))


def dot(a, b):
    return lax.dot_general(a, b, (((1,), (0,)), ((), ())), preferred_element_type=f32)


def dot_nt(a, b):
    return lax.dot_general(a, b, (((1,), (1,)), ((), ())), preferred_element_type=f32)


def dot_tn(a, b):
    return lax.dot_general(a, b, (((0,), (0,)), ((), ())), preferred_element_type=f32)


def route_table(slots, count, token_pos):
    live = jnp.arange(slots.shape[0]) < count
    return ((slots[:, None] == token_pos[None, :]) & live[:, None]).astype(bf16)


def head_windows(width, head):
    found = []
    for low in range(0, width, head):
        first, last = low // LANES, (low + head - 1) // LANES
        found.append((first * LANES, (last + 1) * LANES, low - first * LANES))
    return found


def head_lanes(rows, low, high, offset, head):
    lane = lax.broadcasted_iota(jnp.int32, (rows, high - low), 1)
    return (lane >= offset) & (lane < offset + head)


def add_tiles(tiles, low, values):
    for t in range(values.shape[1] // LANES):
        part = values[:, t * LANES : (t + 1) * LANES]
        k = low // LANES + t
        tiles[k] = part if tiles[k] is None else tiles[k] + part


def attend(q, kv, q_seg, k_seg, head, block, reach, out_type):
    count, width = q.shape
    keys = kv.shape[0]
    span = block + 2 * reach if reach else keys
    windows = head_windows(width, head)
    scale = head ** (-0.5)

    def body(q_ref, kv_ref, q_seg_ref, k_seg_ref, out_ref, prob_ref):
        start = pl.multiple_of(pl.program_id(0) * block, block) if reach else 0
        rows = pl.ds(start, span)
        allowed = q_seg_ref[...] == k_seg_ref[:, rows]
        if reach:
            ahead = lax.broadcasted_iota(jnp.int32, (block, span), 1) - lax.broadcasted_iota(
                jnp.int32, (block, span), 0
            )
            allowed = allowed & (ahead >= 0) & (ahead <= 2 * reach)
        tiles = [None] * (width // LANES)
        for h, (low, high, offset) in enumerate(windows):
            mine = head_lanes(block, low, high, offset, head)
            q_head = jnp.where(mine, q_ref[:, low:high], 0)
            scores = dot_nt(q_head, kv_ref[rows, low:high]) * scale
            scores = jnp.where(allowed, scores, masked_score)
            raised = jnp.exp(scores - jnp.max(scores, axis=-1, keepdims=True))
            probs = (raised * (1.0 / jnp.sum(raised, axis=-1, keepdims=True))).astype(bf16)
            prob_ref[h] = probs
            mixed = dot(probs, kv_ref[rows, width + low : width + high])
            add_tiles(tiles, low, jnp.where(mine, mixed, 0.0))
        for t, tile in enumerate(tiles):
            out_ref[:, t * LANES : (t + 1) * LANES] = tile.astype(out_type)

    return pl.pallas_call(
        body,
        grid=(count // block,),
        in_specs=[
            pl.BlockSpec((block, width), lambda b: (b, 0)),
            pl.BlockSpec((keys, 2 * width), lambda b: (0, 0)),
            pl.BlockSpec((block, 1), lambda b: (b, 0)),
            pl.BlockSpec((1, keys), lambda b: (0, 0)),
        ],
        out_specs=[
            pl.BlockSpec((block, width), lambda b: (b, 0)),
            pl.BlockSpec((len(windows), block, span), lambda b: (0, b, 0)),
        ],
        out_shape=[
            jax.ShapeDtypeStruct((count, width), out_type),
            jax.ShapeDtypeStruct((len(windows), count, span), bf16),
        ],
        compiler_params=pltpu.CompilerParams(vmem_limit_bytes=32 * 2**20),
        cost_estimate=pl.CostEstimate(
            flops=4 * count * span * width,
            transcendentals=len(windows) * count * span,
            bytes_accessed=2 * (2 * count * width + 2 * keys * width + len(windows) * count * span),
        ),
    )(q, kv, q_seg[:, None], k_seg[None])


def attend_back(q, kv, probs, grad, head, block, reach):
    count, width = q.shape
    keys = kv.shape[0]
    span = block + 2 * reach if reach else keys
    windows = head_windows(width, head)
    scale = head ** (-0.5)

    def body(q_ref, kv_ref, prob_ref, grad_ref, q_grad_ref, kv_grad_ref, sums_ref):
        step = pl.program_id(0)

        @pl.when(step == 0)
        def _():
            sums_ref[...] = jnp.zeros_like(sums_ref)

        start = pl.multiple_of(step * block, block) if reach else 0
        rows = pl.ds(start, span)
        tiles = [None] * (width // LANES)
        for h, (low, high, offset) in enumerate(windows):
            mine = head_lanes(block, low, high, offset, head)
            q_head = jnp.where(mine, q_ref[:, low:high], 0)
            g_head = jnp.where(mine, grad_ref[:, low:high], 0)
            p_head = prob_ref[h]
            p_wide = p_head.astype(f32)
            p_grad = dot_nt(g_head, kv_ref[rows, width + low : width + high])
            inner = jnp.sum(p_wide * p_grad, axis=-1, keepdims=True)
            s_grad = (p_wide * (p_grad - inner)).astype(bf16)
            q_part = dot(s_grad, kv_ref[rows, low:high]) * scale
            add_tiles(tiles, low, jnp.where(mine, q_part, 0.0))
            sums_ref[rows, low:high] += dot_tn(s_grad, q_head) * scale
            sums_ref[rows, width + low : width + high] += dot_tn(p_head, g_head)
        for t, tile in enumerate(tiles):
            q_grad_ref[:, t * LANES : (t + 1) * LANES] = tile.astype(bf16)

        @pl.when(step == count // block - 1)
        def _():
            kv_grad_ref[...] = sums_ref[...].astype(bf16)

    return pl.pallas_call(
        body,
        grid=(count // block,),
        in_specs=[
            pl.BlockSpec((block, width), lambda b: (b, 0)),
            pl.BlockSpec((keys, 2 * width), lambda b: (0, 0)),
            pl.BlockSpec((len(windows), block, span), lambda b: (0, b, 0)),
            pl.BlockSpec((block, width), lambda b: (b, 0)),
        ],
        out_specs=[
            pl.BlockSpec((block, width), lambda b: (b, 0)),
            pl.BlockSpec((keys, 2 * width), lambda b: (0, 0)),
        ],
        out_shape=[
            jax.ShapeDtypeStruct((count, width), bf16),
            jax.ShapeDtypeStruct((keys, 2 * width), bf16),
        ],
        scratch_shapes=[pltpu.VMEM((keys, 2 * width), f32)],
        compiler_params=pltpu.CompilerParams(vmem_limit_bytes=40 * 2**20),
        cost_estimate=pl.CostEstimate(
            flops=8 * count * span * width,
            transcendentals=0,
            bytes_accessed=2 * (3 * count * width + 4 * keys * width + len(windows) * count * span),
        ),
    )(q, kv, probs, grad)


def shards(
    layer_input,
    cotangent,
    segment_ids,
    route_index,
    route_count,
    attn_gain,
    light_qkv,
    light_out,
    heavy_qkv,
    heavy_out,
    attn_router,
    ffn_gain,
    light_gate_up,
    light_down,
    heavy_gate_up,
    heavy_down,
    ffn_router,
):
    dp, seq = lax.axis_size("dp"), lax.axis_size("seq")
    pos = lax.axis_index("seq")
    x_in, cot, seg = layer_input[0], cotangent[0], segment_ids[0]
    tokens, width = x_in.shape
    slots, counts = route_index[0], route_count[0]
    routed = slots.shape[1]
    token_pos = pos * tokens + jnp.arange(tokens, dtype=jnp.int32)
    table_q = route_table(slots[0], counts[0], token_pos)
    table_kv = route_table(slots[1], counts[1], token_pos)
    table_f = route_table(slots[2], counts[2], token_pos)

    rows, wide = light_qkv.shape
    unit, light_unit = heavy_down.shape[0], light_down.shape[0]
    light_cut, half = light_gate_up.shape[1], seq // 2
    merged = lambda block: block.reshape(-1, block.shape[-1])
    by_dp = lambda grad: grad.reshape(dp, -1, grad.shape[1])
    by_seq = lambda mine: mine.reshape(seq, rows, -1)
    hops = len(dp_stages(dp))
    odd = pos & 1
    fold_width = width * light_unit // rows

    small = jnp.stack([attn_gain, attn_router, ffn_gain, ffn_router], axis=1)
    first = jnp.concatenate([light_qkv, jnp.pad(small, ((0, 0), (0, LANES - 4)))], axis=1)
    got_first = send_seq(lambda k: first)
    light_ffn_own = jnp.concatenate([light_gate_up, fold(light_down, rows)], axis=1)
    light_ffn_all = lax.all_gather(light_ffn_own, ("dp", "seq"), axis=0, tiled=True)
    marked = jnp.concatenate(
        [x_in, jnp.broadcast_to(seg.astype(bf16)[:, None], (tokens, LANES))], axis=1
    )
    left = lax.ppermute(marked[tokens - WINDOW :], "seq", [(i, i + 1) for i in range(seq - 1)])
    right = lax.ppermute(marked[:WINDOW], "seq", [(i + 1, i) for i in range(seq - 1)])
    kv_part = dot(table_kv, marked).astype(bf16)
    own_gu, other_gu = split_columns(odd[None], heavy_gate_up, unit)
    first_held = {(): place_seq([first] + got_first)[0]}
    wave(first_held, 0)

    others = fence(heavy_qkv, light_out, heavy_out, *got_first)[:3]
    second = jnp.concatenate(others, axis=1)
    sum_kv = Sum(kv_part, *got_first)
    got_second = send_seq(lambda k: second)
    for h in range(1, hops):
        wave(first_held, h, second)
    w_lqkv, small_all = place_dp(first_held, [wide, LANES])

    small_t = small_all[:, :4].T
    gain_attn = small_t[0].astype(f32)[None]
    router_attn = small_t[1][None]
    gain_ffn = small_t[2].astype(f32)[None]
    router_ffn = small_t[3][None]

    ext_marked = jnp.concatenate([left, marked, right], axis=0)
    ext_in = ext_marked[:, :width].astype(f32)
    ext_inv = inv_rms(ext_in)
    normed_ext = (ext_in * ext_inv * gain_attn).astype(bf16)
    normed = normed_ext[WINDOW : WINDOW + tokens]
    place_of = jnp.arange(tokens + 2 * WINDOW) - WINDOW
    outside = ((pos == 0) & (place_of < 0)) | ((pos == seq - 1) & (place_of >= tokens))
    key_seg = jnp.where(outside, -1.0, ext_marked[:, width].astype(f32))
    seg_f = seg.astype(f32)
    light_q = dot(normed, w_lqkv[:, :width]).astype(bf16)
    light_kv = dot(normed_ext, w_lqkv[:, width:]).astype(bf16)
    cot_part = dot(table_f, cot).astype(bf16)

    (second_z,) = place_seq([gate(second, light_kv, light_q)] + got_second)
    second_held = {(): second_z}
    wave(second_held, 0)
    sum_kv.add(light_kv)
    light_mixed, light_probs = attend(
        gate(light_q, second_z, sum_kv.part), light_kv, seg_f, key_seg, L_HEAD, WINDOW, WINDOW, bf16
    )
    q_rows = dot(table_q, normed).astype(bf16)
    q_seg = jnp.sum(table_q.astype(f32) * seg_f[None], axis=1)

    for h in range(1, hops):
        wave(second_held, h, light_mixed)
    kv_marked = sum_kv.finish(light_mixed)
    own_gu, other_gu = fence(own_gu, other_gu, light_mixed)[:2]
    got_gu = send_seq(lambda k: other_gu if k & 1 else own_gu)
    got_down = send_seq(lambda k: gate(heavy_down, light_mixed), 2)
    w_hqkv, w_lout, w_hout = place_dp(second_held, [wide, width, width], light_mixed)
    kv_in = kv_marked[:, :width].astype(f32)
    kv_rows = (kv_in * inv_rms(kv_in) * gain_attn).astype(bf16)
    kv_seg = jnp.where(jnp.arange(routed) < counts[1], kv_marked[:, width].astype(f32), -1.0)
    heavy_q = dot(q_rows, w_hqkv[:, :width]).astype(bf16)
    heavy_kv = dot(kv_rows, w_hqkv[:, width:]).astype(bf16)
    heavy_mixed, heavy_probs = attend(
        heavy_q, heavy_kv, q_seg, kv_seg, H_HEAD, min(routed, 256), 0, f32
    )
    gate_attn = sigmoid(
        jnp.sum(q_rows.astype(f32) * router_attn.astype(f32), axis=1, keepdims=True)
    )
    gated = (gate_attn * heavy_mixed).astype(bf16)
    heavy_rows = dot(gated, w_hout).astype(bf16)
    midway = x_in.astype(f32) + dot(light_mixed, w_lout) + dot_tn(table_q, heavy_rows)
    inv_ffn = inv_rms(midway)
    normed_ffn = (midway * inv_ffn * gain_ffn).astype(bf16)
    rows_part = dot(table_f, normed_ffn).astype(bf16)

    sum_rows = Sum(rows_part, pair=True)
    sum_cot = Sum(cot_part, rows_part, pair=True)
    (gu_z,) = place_seq([gate(own_gu, heavy_mixed)] + got_gu)
    (down_z,) = place([gate(heavy_down, heavy_mixed)] + got_down, seq_order(range(0, seq, 2)) // 2, [width])
    gu_held, down_held = {(): gu_z}, {(): down_z}
    wave(gu_held, 0)
    wave(down_held, 0)
    w_lgu = light_ffn_all[:, :light_cut]
    w_ldown = merged(unfold(light_ffn_all[:, light_cut:].reshape(dp * seq, rows, -1), light_unit, width))

    light_units = w_ldown.shape[0]
    light_pre = dot(normed_ffn, w_lgu)
    light_gate, light_up = light_pre[:, :light_units], light_pre[:, light_units:]
    light_act, light_slope = gelu_both(light_gate)
    light_hidden = (light_act * light_up).astype(bf16)
    light_ffn = dot(light_hidden, w_ldown)
    grad_ldown = dot_tn(light_hidden, cot).astype(bf16)
    hidden_grad = dot_nt(cot, w_ldown).astype(bf16).astype(f32)
    light_pre_grad = jnp.concatenate(
        [hidden_grad * light_up * light_slope, hidden_grad * light_act], axis=-1
    ).astype(bf16)
    grad_lgu = dot_tn(normed_ffn, light_pre_grad).astype(bf16)
    normed_ffn_grad = dot_nt(light_pre_grad, w_lgu)

    grad_ldown = merged(fold(grad_ldown.reshape(dp * seq, -1, width), rows))
    light_sum = lax.psum_scatter(
        jnp.concatenate([grad_lgu, grad_ldown], axis=1), ("dp", "seq"), scatter_dimension=0, tiled=True
    )
    for h in range(1, hops):
        wave(gu_held, h, light_ffn)
        wave(down_held, h, light_ffn)
    ffn_rows = sum_rows.finish(normed_ffn_grad, light_ffn)
    cot_rows = sum_cot.finish(normed_ffn_grad, light_ffn)
    (w_hgu,) = place_dp(gu_held, [gu_z.shape[1]], ffn_rows)
    (w_hdown,) = place_dp(down_held, [width], ffn_rows)

    heavy_units = w_hdown.shape[0]
    heavy_pre = dot(ffn_rows, w_hgu)
    heavy_gate, heavy_up = heavy_pre[:, :heavy_units], heavy_pre[:, heavy_units:]
    heavy_act, heavy_slope = gelu_both(heavy_gate)
    ffn_gate = sigmoid(
        jnp.sum(ffn_rows.astype(f32) * router_ffn.astype(f32), axis=1, keepdims=True)
    )
    heavy_hidden = (ffn_gate * heavy_act * heavy_up).astype(bf16)
    heavy_grad = dot_nt(cot_rows, w_hdown).astype(bf16).astype(f32)
    heavy_pre_grad = jnp.concatenate(
        [heavy_grad * ffn_gate * heavy_up * heavy_slope, heavy_grad * ffn_gate * heavy_act],
        axis=-1,
    ).astype(bf16)
    ffn_score_grad = (
        ffn_gate
        * (1.0 - ffn_gate)
        * jnp.sum(heavy_grad * heavy_act * heavy_up, axis=1, keepdims=True)
    )
    rows_grad_part = dot_nt(heavy_pre_grad, w_hgu) + ffn_score_grad * router_ffn.astype(f32)
    rows_grad = rows_grad_part.astype(bf16)
    sum_rows = Sum(rows_grad, pair=True)
    heavy_hidden, heavy_pre_grad, ffn_score_grad = fence(
        heavy_hidden, heavy_pre_grad, ffn_score_grad, rows_grad
    )[:3]
    grad_ffn_router = jnp.sum(ffn_rows.astype(f32) * ffn_score_grad, axis=0)
    grad_hdown = dot_tn(heavy_hidden, cot_rows).astype(bf16)
    grad_hgu = dot_tn(ffn_rows, heavy_pre_grad).astype(bf16)
    out_part = dot(heavy_hidden, w_hdown).astype(bf16)
    rows_grad = sum_rows.finish(grad_hdown, grad_hgu, out_part)
    sum_heavy = [scatter_dp([by_dp(grad_hgu)]), scatter_dp([by_dp(grad_hdown)])]

    sum_out = Sum(out_part, rows_grad, pair=True)
    normed_ffn_grad = normed_ffn_grad + dot_tn(table_f, rows_grad)
    midway_grad = cot.astype(f32) + norm_back(midway, inv_ffn, normed_ffn_grad * gain_ffn)

    out_grad = midway_grad.astype(bf16)
    for s in sum_heavy:
        s.step(out_grad)
    out_grad = gate(out_grad, *[s.keep for s in sum_heavy])
    grad_lout = dot_tn(light_mixed, out_grad).astype(bf16)
    heavy_out_cot = dot(table_q, out_grad).astype(bf16)
    grad_hout = dot_tn(gated, heavy_out_cot).astype(bf16)
    gated_grad = dot_nt(heavy_out_cot, w_hout).astype(bf16).astype(f32)
    heavy_mixed_grad = (gate_attn * gated_grad).astype(bf16)
    attn_score_grad = gate_attn * (1.0 - gate_attn) * jnp.sum(gated_grad * heavy_mixed, axis=1, keepdims=True)
    heavy_q_grad, heavy_kv_grad = attend_back(
        heavy_q, heavy_kv, heavy_probs, heavy_mixed_grad, H_HEAD, min(routed, 256), 0
    )
    grad_hq = dot_tn(q_rows, heavy_q_grad).astype(bf16)
    grad_hkv = dot_tn(kv_rows, heavy_kv_grad).astype(bf16)
    grad_attn_router = jnp.sum(q_rows.astype(f32) * attn_score_grad, axis=0)
    routers = jnp.pad(
        jnp.stack([grad_attn_router, grad_ffn_router], axis=1), ((0, 0), (0, LANES - 2))
    ).astype(bf16)
    q_rows_grad = (
        dot_nt(heavy_q_grad, w_hqkv[:, :width]) + attn_score_grad * router_attn.astype(f32)
    ).astype(bf16)
    kv_send = dot_nt(heavy_kv_grad, w_hqkv[:, width:]).astype(bf16)
    mixed_grad = dot_nt(out_grad, w_lout).astype(bf16)
    attn_grads = [by_dp(g) for g in (grad_hq, grad_hkv, grad_lout, grad_hout, routers)]

    sum_attn = scatter_dp(attn_grads)
    sum_kv = Sum(kv_send)
    out_part = sum_out.finish(kv_send)
    for s in sum_heavy:
        s.step(kv_send)
    light_q_grad, light_kv_grad = attend_back(
        light_q,
        light_kv,
        light_probs,
        gate(mixed_grad, sum_attn.keep, kv_send, out_part, *[s.keep for s in sum_heavy]),
        L_HEAD,
        WINDOW,
        WINDOW,
    )

    sum_attn.step(light_kv_grad)
    grad_lq = by_dp(dot_tn(normed, light_q_grad).astype(bf16))
    grad_lkv = by_dp(dot_tn(normed_ext, light_kv_grad).astype(bf16))
    sum_last = scatter_dp([grad_lq, grad_lkv])
    heavy_z = by_seq(sum_heavy[0].finish(sum_last.keep)).astype(bf16)
    down_z = sum_heavy[1].finish(sum_last.keep).astype(bf16).reshape(half, unit, width)
    sum_kv.add(grad_lkv)
    got_heavy = [pick_seq(heavy_z)(0)] + send_seq(pick_seq(heavy_z))
    pick_down = lambda k: lax.dynamic_index_in_dim(down_z, (pos ^ k) // 2, 0, keepdims=False)
    got_down = [pick_down(0)] + send_seq(pick_down, 2)
    sum_last.step()
    ext_grad = dot_nt(gate(light_kv_grad, sum_last.keep), w_lqkv[:, width:])
    from_right = lax.ppermute(
        ext_grad[WINDOW + tokens :].astype(bf16), "seq", [(i, i + 1) for i in range(seq - 1)]
    )
    from_left = lax.ppermute(
        ext_grad[:WINDOW].astype(bf16), "seq", [(i + 1, i) for i in range(seq - 1)]
    )
    own_grad = (
        ext_grad[WINDOW : WINDOW + tokens]
        + dot_nt(light_q_grad, w_lqkv[:, :width])
        + dot_tn(table_q, q_rows_grad)
    )
    sum_last.step(own_grad)
    sum_attn.step(own_grad)
    attn_mine = by_seq(sum_attn.finish(own_grad))
    light_last = by_seq(sum_last.finish(attn_mine))
    attn_sent = send_seq(pick_seq(attn_mine.astype(bf16)))
    light_sent = send_seq(pick_seq(light_last.astype(bf16)))
    attn_outs = pick_seq(attn_mine)(0) + sum(g.astype(f32) for g in attn_sent)
    last_mine = light_last
    light_last = light_sent[0]
    kv_total = sum_kv.finish(light_last)
    light_outs = pick_seq(last_mine)(0) + sum(g.astype(f32) for g in light_sent)

    light_sum = gate(light_sum, light_last, ext_grad).astype(f32)
    out_light_gate_up = light_sum[:, :light_cut]
    out_light_down = unfold(light_sum[:, light_cut:], light_unit, width)
    got_heavy = [gate(g, light_last) for g in got_heavy]
    got_down = [gate(g, light_last) for g in got_down]
    out_heavy_down = sum(g.astype(f32) for g in got_down)
    out_heavy_gate_up = join_columns(odd[None], got_heavy, unit)
    midway, out_part = fence(midway, out_part, light_last)[:2]
    layer_output = (midway + light_ffn + dot_tn(table_f, out_part)).astype(bf16)
    out_heavy_qkv = attn_outs[:, :wide]
    out_light_out = attn_outs[:, wide : wide + width]
    out_heavy_out = attn_outs[:, wide + width : wide + 2 * width]
    out_attn_router = attn_outs[:, wide + 2 * width]
    out_ffn_router = attn_outs[:, wide + 2 * width + 1]

    def along(weight, grad):
        return jnp.sum(weight.astype(f32) * grad, axis=1)

    out_attn_gain = (
        along(light_qkv, light_outs)
        + along(heavy_qkv, out_heavy_qkv)
        + attn_router.astype(f32) * out_attn_router
    ) / attn_gain.astype(f32)
    out_ffn_gain = (
        along(light_gate_up, out_light_gate_up)
        + along(heavy_gate_up, out_heavy_gate_up)
        + ffn_router.astype(f32) * out_ffn_router
    ) / ffn_gain.astype(f32)
    edge = jnp.concatenate(
        [from_right.astype(f32), jnp.zeros((tokens - 2 * WINDOW, width), f32), from_left.astype(f32)]
    )
    total_grad = own_grad + edge + dot_tn(table_kv, kv_total)
    x_wide = x_in.astype(f32)
    input_grad = midway_grad + norm_back(
        x_wide, ext_inv[WINDOW : WINDOW + tokens], total_grad * gain_attn
    )

    return (
        layer_output[None],
        input_grad.astype(bf16)[None],
        out_attn_gain,
        light_outs,
        out_light_out,
        out_heavy_qkv,
        out_heavy_out,
        out_attn_router,
        out_ffn_gain,
        out_light_gate_up,
        out_light_down,
        out_heavy_gate_up,
        out_heavy_down,
        out_ffn_router,
    )


def solution(mesh):
    both = ("dp", "seq")
    vector, matrix, tokens = P(both), P(both, None), P("dp", "seq", None)
    return jax.shard_map(
        shards,
        mesh=mesh,
        in_specs=(
            tokens,
            tokens,
            P("dp", "seq"),
            P("dp", None, None),
            P("dp", None),
            vector,
            matrix,
            matrix,
            matrix,
            matrix,
            vector,
            vector,
            matrix,
            matrix,
            matrix,
            matrix,
            vector,
        ),
        out_specs=(
            tokens,
            tokens,
            vector,
            matrix,
            matrix,
            matrix,
            matrix,
            vector,
            vector,
            matrix,
            matrix,
            matrix,
            matrix,
            vector,
        ),
        check_vma=False,
    )
```

```python
import jax
import jax.numpy as jnp
from jax import lax
from jax.experimental import pallas as pl
from jax.experimental.pallas import tpu as pltpu
from jax.sharding import PartitionSpec as P

L_HEADS = 8
L_HEAD = 96
H_HEADS = 12
H_HEAD = 64
WINDOW = 128
LANES = 128

epsilon = 1e-06
masked_score = -1e30
gelu_scale = 0.7978845608028654
bf16 = jnp.bfloat16
f32 = jnp.float32


def dma_moves(index, arrays, out_shapes, moves):
    def body(index_ref, *refs):
        ins, outs, sems = refs[: len(arrays)], refs[len(arrays) : -1], refs[-1]
        copies = [
            pltpu.make_async_copy(source(ins, index_ref), target(outs, index_ref), sems.at[k])
            for k, (source, target) in enumerate(moves)
        ]
        for copy in copies:
            copy.start()
        for copy in copies:
            copy.wait()

    return pl.pallas_call(
        body,
        out_shape=[jax.ShapeDtypeStruct(s, a) for s, a in out_shapes],
        in_specs=[pl.BlockSpec(memory_space=pltpu.SMEM)]
        + [pl.BlockSpec(memory_space=pl.ANY)] * len(arrays),
        out_specs=[pl.BlockSpec(memory_space=pltpu.VMEM)] * len(out_shapes),
        scratch_shapes=[pltpu.SemaphoreType.DMA((len(moves),))],
        compiler_params=pltpu.CompilerParams(vmem_limit_bytes=16 * 2**20),
    )(index, *arrays)


def dp_stages(count):
    if count == 8:
        return [
            lambda i: i ^ (2 + 2 * (i & 1)),
            lambda i: i ^ (4 - 2 * (i & 1)),
            lambda i: i ^ 1,
        ]
    masks = [1 << b for b in range(count.bit_length() - 1)][::-1]
    return [lambda i, m=m: i ^ m for m in masks]


def dp_labels(count):
    labels = [()]
    for stage in range(len(dp_stages(count))):
        labels = labels + [label + (stage,) for label in labels]
    return labels


def dp_order():
    count, me = lax.axis_size("dp"), lax.axis_index("dp")
    stages = dp_stages(count)

    def source(label):
        at = me
        for stage in label[::-1]:
            at = stages[stage](at)
        return at

    return jnp.stack([source(label) for label in dp_labels(count)]).astype(jnp.int32)


def perm(count, stage):
    return [(i, stage(i)) for i in range(count)]


def perm_seq(count, k):
    return [(i, i ^ k) for i in range(count)]


def fence(*values):
    return lax.optimization_barrier(values) if len(values) > 1 else values


def gate(value, *others):
    return lax.optimization_barrier((value,) + others)[0] if others else value


def seq_order(steps):
    pos = lax.axis_index("seq")
    return jnp.stack([pos ^ k for k in steps]).astype(jnp.int32)


def place_seq(pieces, widths=None):
    return place(pieces, seq_order(range(len(pieces))), widths or [pieces[0].shape[-1]])


def place(pieces, order, widths):
    count, lead = len(pieces), pieces[0].shape[:-1]
    moves, shapes, low = [], [], 0
    for j, columns in enumerate(widths):
        shapes.append(((count,) + lead + (columns,), bf16))
        for k in range(count):
            moves.append(
                (
                    lambda ins, idx, k=k, low=low, columns=columns: ins[k].at[
                        ..., pl.ds(low, columns)
                    ],
                    lambda outs, idx, k=k, j=j: outs[j].at[idx[k]],
                )
            )
        low += columns
    return [p.reshape(-1, p.shape[-1]) for p in dma_moves(order, pieces, shapes, moves)]


def fold(block, rows):
    count, width = block.shape[-2:]
    extra = count - rows
    if not extra:
        return block
    if rows % 8 or extra % 8 or extra < 0 or rows % extra or width % (rows // extra * LANES):
        return block.reshape(block.shape[:-2] + (rows, -1))
    groups = jnp.split(block[..., rows:, :], rows // extra, axis=-1)
    return jnp.concatenate([block[..., :rows, :], jnp.concatenate(groups, axis=-2)], axis=-1)


def unfold(block, count, width):
    rows = block.shape[-2]
    extra = count - rows
    if not extra:
        return block
    if rows % 8 or extra % 8 or extra < 0 or rows % extra or width % (rows // extra * LANES):
        return block.reshape(block.shape[:-2] + (count, width))
    groups = jnp.split(block[..., width:], rows // extra, axis=-2)
    return jnp.concatenate([block[..., :width], jnp.concatenate(groups, axis=-1)], axis=-2)


def send_seq(piece_for, every=1):
    count = lax.axis_size("seq")
    steps = range(every, count, every)
    return [lax.ppermute(piece_for(k), "seq", perm_seq(count, k)) for k in steps]


def wave(pieces, hops, *after):
    count = lax.axis_size("dp")
    stages = dp_stages(count)
    for label in [p for p in pieces if len(p) == hops]:
        later = range(label[-1] + 1 if label else 0, len(stages))
        if len(later):
            pieces[label] = gate(pieces[label], *after)
        for stage in later:
            pieces[label + (stage,)] = lax.ppermute(
                pieces[label], "dp", perm(count, stages[stage])
            )


def place_dp(held, widths, *after):
    pieces = [held[label] for label in dp_labels(lax.axis_size("dp"))]
    return place(pieces, gate(dp_order(), *after), widths)


def scatter_dp(grads):
    count = lax.axis_size("dp")
    half = count // 2
    rows = grads[0].shape[1]
    width = sum(g.shape[2] for g in grads)
    moves, low = [], 0
    for j, grad in enumerate(grads):
        columns = grad.shape[2]
        for k in range(count):
            moves.append(
                (
                    lambda ins, idx, k=k, j=j: ins[j].at[idx[k]],
                    lambda outs, idx, k=k, low=low, columns=columns: outs[k // half].at[
                        k % half, :, pl.ds(low, columns)
                    ],
                )
            )
        low += columns
    shape = (half, rows, width)
    keep, send = dma_moves(dp_order(), grads, [(shape, bf16), (shape, bf16)], moves)
    return Scatter(keep, send)


class Scatter:
    def __init__(self, keep, send):
        self.keep, self.left = keep, dp_stages(lax.axis_size("dp"))
        self.hop(send)

    def hop(self, send):
        count = lax.axis_size("dp")
        self.got = lax.ppermute(send, "dp", perm(count, self.left.pop()))

    def step(self, *after):
        self.keep = gate(self.keep, *after)
        half = self.keep.shape[0] // 2
        wide = lambda part: part.astype(f32)
        send = (wide(self.keep[half:]) + wide(self.got[half:])).astype(bf16)
        self.keep = (wide(self.keep[:half]) + wide(self.got[:half])).astype(bf16)
        self.hop(send)

    def finish(self, *after):
        while len(self.left):
            self.step(*after)
        return gate(self.keep, *after)[0].astype(f32) + self.got[0].astype(f32)


def pick_seq(blocks):
    pos = lax.axis_index("seq")
    return lambda k: lax.dynamic_index_in_dim(blocks, pos ^ k, 0, keepdims=False)


class Sum:
    def __init__(self, part, *after, pair=False):
        self.masks = [1 << b for b in range(lax.axis_size("seq").bit_length() - 1)]
        if pair:
            self.masks = self.masks[:1]
        self.part = gate(part, *after)
        self.send()

    def send(self):
        pairs = perm_seq(lax.axis_size("seq"), self.masks.pop(0))
        self.got = lax.ppermute(self.part, "seq", pairs)

    def add(self, *after):
        part = gate(self.part, *after)
        self.part = (part.astype(f32) + self.got.astype(f32)).astype(bf16)
        if self.masks:
            self.send()

    def finish(self, *after):
        while self.masks:
            self.add(*after)
        self.add(*after)
        return self.part


def split_columns(odd, weights, chunk):
    rows, width = weights.shape
    pairs = width // (2 * chunk)

    def body(odd_ref, weights_ref, own_ref, other_ref):
        def copy(own, other):
            for j in range(pairs):
                at = pl.ds(j * chunk, chunk)
                own[:, at] = weights_ref[:, pl.ds(2 * j * chunk, chunk)]
                other[:, at] = weights_ref[:, pl.ds((2 * j + 1) * chunk, chunk)]

        @pl.when(odd_ref[0] == 0)
        def _():
            copy(own_ref, other_ref)

        @pl.when(odd_ref[0] == 1)
        def _():
            copy(other_ref, own_ref)

    return pl.pallas_call(
        body,
        in_specs=[pl.BlockSpec(memory_space=pltpu.SMEM), pl.BlockSpec(memory_space=pltpu.VMEM)],
        out_specs=[pl.BlockSpec(memory_space=pltpu.VMEM)] * 2,
        out_shape=[jax.ShapeDtypeStruct((rows, width // 2), weights.dtype)] * 2,
    )(odd, weights)


def join_columns(odd, pieces, chunk):
    rows, width = pieces[0].shape
    count = len(pieces)

    def body(odd_ref, *refs):
        out_ref = refs[-1]

        def fill(first, second):
            for j in range(width // chunk):
                at = pl.ds(j * chunk, chunk)
                for side, group in enumerate((first, second)):
                    total = group[0][:, at].astype(f32)
                    for ref in group[1:]:
                        total = total + ref[:, at].astype(f32)
                    out_ref[:, pl.ds((2 * j + side) * chunk, chunk)] = total

        @pl.when(odd_ref[0] == 0)
        def _():
            fill(refs[0:count:2], refs[1:count:2])

        @pl.when(odd_ref[0] == 1)
        def _():
            fill(refs[1:count:2], refs[0:count:2])

    return pl.pallas_call(
        body,
        in_specs=[pl.BlockSpec(memory_space=pltpu.SMEM)]
        + [pl.BlockSpec(memory_space=pltpu.VMEM)] * count,
        out_specs=pl.BlockSpec(memory_space=pltpu.VMEM),
        out_shape=jax.ShapeDtypeStruct((rows, 2 * width), f32),
    )(odd, *pieces)


def inv_rms(values):
    return lax.rsqrt(jnp.mean(values * values, axis=-1, keepdims=True) + epsilon)


def norm_back(values, inv, scaled):
    inner = jnp.mean(scaled * values, axis=-1, keepdims=True)
    return inv * scaled - values * (inv * inv * inv) * inner


def gelu_both(v):
    inner = jnp.tanh(gelu_scale * (v + 0.044715 * v * v * v))
    value = 0.5 * v * (1.0 + inner)
    slope = 0.5 * (1.0 + inner) + 0.5 * v * (1.0 - inner * inner) * gelu_scale * (
        1.0 + 3.0 * 0.044715 * v * v
    )
    return value, slope


def sigmoid(values):
    return 1.0 / (1.0 + jnp.exp(-values))


def dot(a, b):
    return lax.dot_general(a, b, (((1,), (0,)), ((), ())), preferred_element_type=f32)


def dot_nt(a, b):
    return lax.dot_general(a, b, (((1,), (1,)), ((), ())), preferred_element_type=f32)


def dot_tn(a, b):
    return lax.dot_general(a, b, (((0,), (0,)), ((), ())), preferred_element_type=f32)


def route_table(slots, count, token_pos):
    live = jnp.arange(slots.shape[0]) < count
    return ((slots[:, None] == token_pos[None, :]) & live[:, None]).astype(bf16)


def head_windows(width, head):
    found = []
    for low in range(0, width, head):
        first, last = low // LANES, (low + head - 1) // LANES
        found.append((first * LANES, (last + 1) * LANES, low - first * LANES))
    return found


def head_lanes(rows, low, high, offset, head):
    lane = lax.broadcasted_iota(jnp.int32, (rows, high - low), 1)
    return (lane >= offset) & (lane < offset + head)


def add_tiles(tiles, low, values):
    for t in range(values.shape[1] // LANES):
        part = values[:, t * LANES : (t + 1) * LANES]
        k = low // LANES + t
        tiles[k] = part if tiles[k] is None else tiles[k] + part


def attend(q, kv, q_seg, k_seg, head, block, reach, out_type):
    count, width = q.shape
    keys = kv.shape[0]
    span = block + 2 * reach if reach else keys
    windows = head_windows(width, head)
    scale = head ** (-0.5)

    def body(q_ref, kv_ref, q_seg_ref, k_seg_ref, out_ref, prob_ref):
        start = pl.multiple_of(pl.program_id(0) * block, block) if reach else 0
        rows = pl.ds(start, span)
        allowed = q_seg_ref[...] == k_seg_ref[:, rows]
        if reach:
            ahead = lax.broadcasted_iota(jnp.int32, (block, span), 1) - lax.broadcasted_iota(
                jnp.int32, (block, span), 0
            )
            allowed = allowed & (ahead >= 0) & (ahead <= 2 * reach)
        tiles = [None] * (width // LANES)
        for h, (low, high, offset) in enumerate(windows):
            mine = head_lanes(block, low, high, offset, head)
            q_head = jnp.where(mine, q_ref[:, low:high], 0)
            scores = dot_nt(q_head, kv_ref[rows, low:high]) * scale
            scores = jnp.where(allowed, scores, masked_score)
            raised = jnp.exp(scores - jnp.max(scores, axis=-1, keepdims=True))
            probs = (raised * (1.0 / jnp.sum(raised, axis=-1, keepdims=True))).astype(bf16)
            prob_ref[h] = probs
            mixed = dot(probs, kv_ref[rows, width + low : width + high])
            add_tiles(tiles, low, jnp.where(mine, mixed, 0.0))
        for t, tile in enumerate(tiles):
            out_ref[:, t * LANES : (t + 1) * LANES] = tile.astype(out_type)

    return pl.pallas_call(
        body,
        grid=(count // block,),
        in_specs=[
            pl.BlockSpec((block, width), lambda b: (b, 0)),
            pl.BlockSpec((keys, 2 * width), lambda b: (0, 0)),
            pl.BlockSpec((block, 1), lambda b: (b, 0)),
            pl.BlockSpec((1, keys), lambda b: (0, 0)),
        ],
        out_specs=[
            pl.BlockSpec((block, width), lambda b: (b, 0)),
            pl.BlockSpec((len(windows), block, span), lambda b: (0, b, 0)),
        ],
        out_shape=[
            jax.ShapeDtypeStruct((count, width), out_type),
            jax.ShapeDtypeStruct((len(windows), count, span), bf16),
        ],
        compiler_params=pltpu.CompilerParams(vmem_limit_bytes=32 * 2**20),
        cost_estimate=pl.CostEstimate(
            flops=4 * count * span * width,
            transcendentals=len(windows) * count * span,
            bytes_accessed=2 * (2 * count * width + 2 * keys * width + len(windows) * count * span),
        ),
    )(q, kv, q_seg[:, None], k_seg[None])


def attend_back(q, kv, probs, grad, head, block, reach):
    count, width = q.shape
    keys = kv.shape[0]
    span = block + 2 * reach if reach else keys
    windows = head_windows(width, head)
    scale = head ** (-0.5)

    def body(q_ref, kv_ref, prob_ref, grad_ref, q_grad_ref, kv_grad_ref, sums_ref):
        step = pl.program_id(0)

        @pl.when(step == 0)
        def _():
            sums_ref[...] = jnp.zeros_like(sums_ref)

        start = pl.multiple_of(step * block, block) if reach else 0
        rows = pl.ds(start, span)
        tiles = [None] * (width // LANES)
        for h, (low, high, offset) in enumerate(windows):
            mine = head_lanes(block, low, high, offset, head)
            q_head = jnp.where(mine, q_ref[:, low:high], 0)
            g_head = jnp.where(mine, grad_ref[:, low:high], 0)
            p_head = prob_ref[h]
            p_wide = p_head.astype(f32)
            p_grad = dot_nt(g_head, kv_ref[rows, width + low : width + high])
            inner = jnp.sum(p_wide * p_grad, axis=-1, keepdims=True)
            s_grad = (p_wide * (p_grad - inner)).astype(bf16)
            q_part = dot(s_grad, kv_ref[rows, low:high]) * scale
            add_tiles(tiles, low, jnp.where(mine, q_part, 0.0))
            sums_ref[rows, low:high] += dot_tn(s_grad, q_head) * scale
            sums_ref[rows, width + low : width + high] += dot_tn(p_head, g_head)
        for t, tile in enumerate(tiles):
            q_grad_ref[:, t * LANES : (t + 1) * LANES] = tile.astype(bf16)

        @pl.when(step == count // block - 1)
        def _():
            kv_grad_ref[...] = sums_ref[...].astype(bf16)

    return pl.pallas_call(
        body,
        grid=(count // block,),
        in_specs=[
            pl.BlockSpec((block, width), lambda b: (b, 0)),
            pl.BlockSpec((keys, 2 * width), lambda b: (0, 0)),
            pl.BlockSpec((len(windows), block, span), lambda b: (0, b, 0)),
            pl.BlockSpec((block, width), lambda b: (b, 0)),
        ],
        out_specs=[
            pl.BlockSpec((block, width), lambda b: (b, 0)),
            pl.BlockSpec((keys, 2 * width), lambda b: (0, 0)),
        ],
        out_shape=[
            jax.ShapeDtypeStruct((count, width), bf16),
            jax.ShapeDtypeStruct((keys, 2 * width), bf16),
        ],
        scratch_shapes=[pltpu.VMEM((keys, 2 * width), f32)],
        compiler_params=pltpu.CompilerParams(vmem_limit_bytes=40 * 2**20),
        cost_estimate=pl.CostEstimate(
            flops=8 * count * span * width,
            transcendentals=0,
            bytes_accessed=2 * (3 * count * width + 4 * keys * width + len(windows) * count * span),
        ),
    )(q, kv, probs, grad)


def shards(
    layer_input,
    cotangent,
    segment_ids,
    route_index,
    route_count,
    attn_gain,
    light_qkv,
    light_out,
    heavy_qkv,
    heavy_out,
    attn_router,
    ffn_gain,
    light_gate_up,
    light_down,
    heavy_gate_up,
    heavy_down,
    ffn_router,
):
    dp, seq = lax.axis_size("dp"), lax.axis_size("seq")
    pos = lax.axis_index("seq")
    x_in, cot, seg = layer_input[0], cotangent[0], segment_ids[0]
    tokens, width = x_in.shape
    slots, counts = route_index[0], route_count[0]
    routed = slots.shape[1]
    token_pos = pos * tokens + jnp.arange(tokens, dtype=jnp.int32)
    table_q = route_table(slots[0], counts[0], token_pos)
    table_kv = route_table(slots[1], counts[1], token_pos)
    table_f = route_table(slots[2], counts[2], token_pos)

    rows, wide = light_qkv.shape
    unit, light_unit = heavy_down.shape[0], light_down.shape[0]
    light_cut, half = light_gate_up.shape[1], seq // 2
    merged = lambda block: block.reshape(-1, block.shape[-1])
    by_dp = lambda grad: grad.reshape(dp, -1, grad.shape[1])
    by_seq = lambda mine: mine.reshape(seq, rows, -1)
    hops = len(dp_stages(dp))
    odd = pos & 1
    fold_width = width * light_unit // rows

    small = jnp.stack([attn_gain, attn_router, ffn_gain, ffn_router], axis=1)
    first = jnp.concatenate([light_qkv, jnp.pad(small, ((0, 0), (0, LANES - 4)))], axis=1)
    got_first = send_seq(lambda k: first)
    light_ffn_own = jnp.concatenate([light_gate_up, fold(light_down, rows)], axis=1)
    light_ffn_all = lax.all_gather(light_ffn_own, ("dp", "seq"), axis=0, tiled=True)
    marked = jnp.concatenate(
        [x_in, jnp.broadcast_to(seg.astype(bf16)[:, None], (tokens, LANES))], axis=1
    )
    left = lax.ppermute(marked[tokens - WINDOW :], "seq", [(i, i + 1) for i in range(seq - 1)])
    right = lax.ppermute(marked[:WINDOW], "seq", [(i + 1, i) for i in range(seq - 1)])
    kv_part = dot(table_kv, marked).astype(bf16)
    own_gu, other_gu = split_columns(odd[None], heavy_gate_up, unit)
    first_held = {(): place_seq([first] + got_first)[0]}
    wave(first_held, 0)

    others = fence(heavy_qkv, light_out, heavy_out, *got_first)[:3]
    second = jnp.concatenate(others, axis=1)
    sum_kv = Sum(kv_part, *got_first)
    got_second = send_seq(lambda k: second)
    for h in range(1, hops):
        wave(first_held, h, second)
    w_lqkv, small_all = place_dp(first_held, [wide, LANES])

    small_t = small_all[:, :4].T
    gain_attn = small_t[0].astype(f32)[None]
    router_attn = small_t[1][None]
    gain_ffn = small_t[2].astype(f32)[None]
    router_ffn = small_t[3][None]

    ext_marked = jnp.concatenate([left, marked, right], axis=0)
    ext_in = ext_marked[:, :width].astype(f32)
    ext_inv = inv_rms(ext_in)
    normed_ext = (ext_in * ext_inv * gain_attn).astype(bf16)
    normed = normed_ext[WINDOW : WINDOW + tokens]
    place_of = jnp.arange(tokens + 2 * WINDOW) - WINDOW
    outside = ((pos == 0) & (place_of < 0)) | ((pos == seq - 1) & (place_of >= tokens))
    key_seg = jnp.where(outside, -1.0, ext_marked[:, width].astype(f32))
    seg_f = seg.astype(f32)
    light_q = dot(normed, w_lqkv[:, :width]).astype(bf16)
    light_kv = dot(normed_ext, w_lqkv[:, width:]).astype(bf16)
    cot_part = dot(table_f, cot).astype(bf16)

    (second_z,) = place_seq([gate(second, light_kv, light_q)] + got_second)
    second_held = {(): second_z}
    wave(second_held, 0)
    sum_kv.add(light_kv)
    light_mixed, light_probs = attend(
        gate(light_q, second_z), light_kv, seg_f, key_seg, L_HEAD, WINDOW, WINDOW, bf16
    )
    q_rows = dot(table_q, normed).astype(bf16)
    q_seg = jnp.sum(table_q.astype(f32) * seg_f[None], axis=1)

    for h in range(1, hops):
        wave(second_held, h, light_mixed)
    kv_marked = sum_kv.finish(light_mixed)
    own_gu, other_gu = fence(own_gu, other_gu, light_mixed)[:2]
    got_gu = send_seq(lambda k: other_gu if k & 1 else own_gu)
    got_down = send_seq(lambda k: gate(heavy_down, light_mixed), 2)
    w_hqkv, w_lout, w_hout = place_dp(second_held, [wide, width, width], light_mixed)
    kv_in = kv_marked[:, :width].astype(f32)
    kv_rows = (kv_in * inv_rms(kv_in) * gain_attn).astype(bf16)
    kv_seg = jnp.where(jnp.arange(routed) < counts[1], kv_marked[:, width].astype(f32), -1.0)
    heavy_q = dot(q_rows, w_hqkv[:, :width]).astype(bf16)
    heavy_kv = dot(kv_rows, w_hqkv[:, width:]).astype(bf16)
    heavy_mixed, heavy_probs = attend(
        heavy_q, heavy_kv, q_seg, kv_seg, H_HEAD, min(routed, 256), 0, f32
    )
    gate_attn = sigmoid(
        jnp.sum(q_rows.astype(f32) * router_attn.astype(f32), axis=1, keepdims=True)
    )
    gated = (gate_attn * heavy_mixed).astype(bf16)
    heavy_rows = dot(gated, w_hout).astype(bf16)
    midway = x_in.astype(f32) + dot(light_mixed, w_lout) + dot_tn(table_q, heavy_rows)
    inv_ffn = inv_rms(midway)
    normed_ffn = (midway * inv_ffn * gain_ffn).astype(bf16)
    rows_part = dot(table_f, normed_ffn).astype(bf16)

    sum_rows = Sum(rows_part, pair=True)
    sum_cot = Sum(cot_part, rows_part, pair=True)
    (gu_z,) = place_seq([gate(own_gu, heavy_mixed)] + got_gu)
    (down_z,) = place([gate(heavy_down, heavy_mixed)] + got_down, seq_order(range(0, seq, 2)) // 2, [width])
    gu_held, down_held = {(): gu_z}, {(): down_z}
    wave(gu_held, 0)
    wave(down_held, 0)
    w_lgu = light_ffn_all[:, :light_cut]
    w_ldown = merged(unfold(light_ffn_all[:, light_cut:].reshape(dp * seq, rows, -1), light_unit, width))

    light_units = w_ldown.shape[0]
    light_pre = dot(normed_ffn, w_lgu)
    light_gate, light_up = light_pre[:, :light_units], light_pre[:, light_units:]
    light_act, light_slope = gelu_both(light_gate)
    light_hidden = (light_act * light_up).astype(bf16)
    light_ffn = dot(light_hidden, w_ldown)
    grad_ldown = dot_tn(light_hidden, cot).astype(bf16)
    hidden_grad = dot_nt(cot, w_ldown).astype(bf16).astype(f32)
    light_pre_grad = jnp.concatenate(
        [hidden_grad * light_up * light_slope, hidden_grad * light_act], axis=-1
    ).astype(bf16)
    grad_lgu = dot_tn(normed_ffn, light_pre_grad).astype(bf16)
    normed_ffn_grad = dot_nt(light_pre_grad, w_lgu)

    grad_ldown = merged(fold(grad_ldown.reshape(dp * seq, -1, width), rows))
    light_sum = lax.psum_scatter(
        jnp.concatenate([grad_lgu, grad_ldown], axis=1), ("dp", "seq"), scatter_dimension=0, tiled=True
    )
    for h in range(1, hops):
        wave(gu_held, h, light_ffn)
        wave(down_held, h, light_ffn)
    ffn_rows = sum_rows.finish(normed_ffn_grad, light_ffn)
    cot_rows = sum_cot.finish(normed_ffn_grad, light_ffn)
    (w_hgu,) = place_dp(gu_held, [gu_z.shape[1]], ffn_rows)
    (w_hdown,) = place_dp(down_held, [width], ffn_rows)

    heavy_units = w_hdown.shape[0]
    heavy_pre = dot(ffn_rows, w_hgu)
    heavy_gate, heavy_up = heavy_pre[:, :heavy_units], heavy_pre[:, heavy_units:]
    heavy_act, heavy_slope = gelu_both(heavy_gate)
    ffn_gate = sigmoid(
        jnp.sum(ffn_rows.astype(f32) * router_ffn.astype(f32), axis=1, keepdims=True)
    )
    heavy_hidden = (ffn_gate * heavy_act * heavy_up).astype(bf16)
    heavy_grad = dot_nt(cot_rows, w_hdown).astype(bf16).astype(f32)
    heavy_pre_grad = jnp.concatenate(
        [heavy_grad * ffn_gate * heavy_up * heavy_slope, heavy_grad * ffn_gate * heavy_act],
        axis=-1,
    ).astype(bf16)
    ffn_score_grad = (
        ffn_gate
        * (1.0 - ffn_gate)
        * jnp.sum(heavy_grad * heavy_act * heavy_up, axis=1, keepdims=True)
    )
    rows_grad_part = dot_nt(heavy_pre_grad, w_hgu) + ffn_score_grad * router_ffn.astype(f32)
    rows_grad = rows_grad_part.astype(bf16)
    sum_rows = Sum(rows_grad, pair=True)
    heavy_hidden, heavy_pre_grad, ffn_score_grad = fence(
        heavy_hidden, heavy_pre_grad, ffn_score_grad, rows_grad
    )[:3]
    grad_ffn_router = jnp.sum(ffn_rows.astype(f32) * ffn_score_grad, axis=0)
    grad_hdown = dot_tn(heavy_hidden, cot_rows).astype(bf16)
    grad_hgu = dot_tn(ffn_rows, heavy_pre_grad).astype(bf16)
    out_part = dot(heavy_hidden, w_hdown).astype(bf16)
    rows_grad = sum_rows.finish(grad_hdown, grad_hgu, out_part)
    sum_heavy = [scatter_dp([by_dp(grad_hgu)]), scatter_dp([by_dp(grad_hdown)])]

    sum_out = Sum(out_part, rows_grad, pair=True)
    normed_ffn_grad = normed_ffn_grad + dot_tn(table_f, rows_grad)
    midway_grad = cot.astype(f32) + norm_back(midway, inv_ffn, normed_ffn_grad * gain_ffn)

    out_grad = midway_grad.astype(bf16)
    for s in sum_heavy:
        s.step(out_grad)
    out_grad = gate(out_grad, *[s.keep for s in sum_heavy])
    grad_lout = dot_tn(light_mixed, out_grad).astype(bf16)
    heavy_out_cot = dot(table_q, out_grad).astype(bf16)
    grad_hout = dot_tn(gated, heavy_out_cot).astype(bf16)
    gated_grad = dot_nt(heavy_out_cot, w_hout).astype(bf16).astype(f32)
    heavy_mixed_grad = (gate_attn * gated_grad).astype(bf16)
    attn_score_grad = gate_attn * (1.0 - gate_attn) * jnp.sum(gated_grad * heavy_mixed, axis=1, keepdims=True)
    heavy_q_grad, heavy_kv_grad = attend_back(
        heavy_q, heavy_kv, heavy_probs, heavy_mixed_grad, H_HEAD, min(routed, 256), 0
    )
    grad_hq = dot_tn(q_rows, heavy_q_grad).astype(bf16)
    grad_hkv = dot_tn(kv_rows, heavy_kv_grad).astype(bf16)
    grad_attn_router = jnp.sum(q_rows.astype(f32) * attn_score_grad, axis=0)
    routers = jnp.pad(
        jnp.stack([grad_attn_router, grad_ffn_router], axis=1), ((0, 0), (0, LANES - 2))
    ).astype(bf16)
    q_rows_grad = (
        dot_nt(heavy_q_grad, w_hqkv[:, :width]) + attn_score_grad * router_attn.astype(f32)
    ).astype(bf16)
    kv_send = dot_nt(heavy_kv_grad, w_hqkv[:, width:]).astype(bf16)
    mixed_grad = dot_nt(out_grad, w_lout).astype(bf16)
    attn_grads = [by_dp(g) for g in (grad_hq, grad_hkv, grad_lout, grad_hout, routers)]

    sum_attn = scatter_dp(attn_grads)
    sum_kv = Sum(kv_send)
    out_part = sum_out.finish(kv_send)
    for s in sum_heavy:
        s.step(kv_send)
    light_q_grad, light_kv_grad = attend_back(
        light_q,
        light_kv,
        light_probs,
        gate(mixed_grad, sum_attn.keep, kv_send, out_part),
        L_HEAD,
        WINDOW,
        WINDOW,
    )

    sum_attn.step(light_kv_grad)
    grad_lq = by_dp(dot_tn(normed, light_q_grad).astype(bf16))
    grad_lkv = by_dp(dot_tn(normed_ext, light_kv_grad).astype(bf16))
    sum_last = scatter_dp([grad_lq, grad_lkv])
    heavy_z = by_seq(sum_heavy[0].finish(sum_last.keep)).astype(bf16)
    down_z = sum_heavy[1].finish(sum_last.keep).astype(bf16).reshape(half, unit, width)
    sum_kv.add(grad_lkv)
    got_heavy = [pick_seq(heavy_z)(0)] + send_seq(pick_seq(heavy_z))
    pick_down = lambda k: lax.dynamic_index_in_dim(down_z, (pos ^ k) // 2, 0, keepdims=False)
    got_down = [pick_down(0)] + send_seq(pick_down, 2)
    sum_last.step()
    ext_grad = dot_nt(gate(light_kv_grad, sum_last.keep), w_lqkv[:, width:])
    from_right = lax.ppermute(
        ext_grad[WINDOW + tokens :].astype(bf16), "seq", [(i, i + 1) for i in range(seq - 1)]
    )
    from_left = lax.ppermute(
        ext_grad[:WINDOW].astype(bf16), "seq", [(i + 1, i) for i in range(seq - 1)]
    )
    own_grad = (
        ext_grad[WINDOW : WINDOW + tokens]
        + dot_nt(light_q_grad, w_lqkv[:, :width])
        + dot_tn(table_q, q_rows_grad)
    )
    sum_last.step(own_grad)
    sum_attn.step(own_grad)
    attn_mine = by_seq(sum_attn.finish(own_grad))
    light_last = by_seq(sum_last.finish(attn_mine))
    attn_sent = send_seq(pick_seq(attn_mine.astype(bf16)))
    light_sent = send_seq(pick_seq(light_last.astype(bf16)))
    attn_outs = pick_seq(attn_mine)(0) + sum(g.astype(f32) for g in attn_sent)
    last_mine = light_last
    light_last = light_sent[0]
    kv_total = sum_kv.finish(light_last)
    light_outs = pick_seq(last_mine)(0) + sum(g.astype(f32) for g in light_sent)

    light_sum = gate(light_sum, light_last, ext_grad).astype(f32)
    out_light_gate_up = light_sum[:, :light_cut]
    out_light_down = unfold(light_sum[:, light_cut:], light_unit, width)
    got_heavy = [gate(g, light_last) for g in got_heavy]
    got_down = [gate(g, light_last) for g in got_down]
    out_heavy_down = sum(g.astype(f32) for g in got_down)
    out_heavy_gate_up = join_columns(odd[None], got_heavy, unit)
    midway, out_part = fence(midway, out_part, light_last)[:2]
    layer_output = (midway + light_ffn + dot_tn(table_f, out_part)).astype(bf16)
    out_heavy_qkv = attn_outs[:, :wide]
    out_light_out = attn_outs[:, wide : wide + width]
    out_heavy_out = attn_outs[:, wide + width : wide + 2 * width]
    out_attn_router = attn_outs[:, wide + 2 * width]
    out_ffn_router = attn_outs[:, wide + 2 * width + 1]

    def along(weight, grad):
        return jnp.sum(weight.astype(f32) * grad, axis=1)

    out_attn_gain = (
        along(light_qkv, light_outs)
        + along(heavy_qkv, out_heavy_qkv)
        + attn_router.astype(f32) * out_attn_router
    ) / attn_gain.astype(f32)
    out_ffn_gain = (
        along(light_gate_up, out_light_gate_up)
        + along(heavy_gate_up, out_heavy_gate_up)
        + ffn_router.astype(f32) * out_ffn_router
    ) / ffn_gain.astype(f32)
    edge = jnp.concatenate(
        [from_right.astype(f32), jnp.zeros((tokens - 2 * WINDOW, width), f32), from_left.astype(f32)]
    )
    total_grad = own_grad + edge + dot_tn(table_kv, kv_total)
    x_wide = x_in.astype(f32)
    input_grad = midway_grad + norm_back(
        x_wide, ext_inv[WINDOW : WINDOW + tokens], total_grad * gain_attn
    )

    return (
        layer_output[None],
        input_grad.astype(bf16)[None],
        out_attn_gain,
        light_outs,
        out_light_out,
        out_heavy_qkv,
        out_heavy_out,
        out_attn_router,
        out_ffn_gain,
        out_light_gate_up,
        out_light_down,
        out_heavy_gate_up,
        out_heavy_down,
        out_ffn_router,
    )


def solution(mesh):
    both = ("dp", "seq")
    vector, matrix, tokens = P(both), P(both, None), P("dp", "seq", None)
    return jax.shard_map(
        shards,
        mesh=mesh,
        in_specs=(
            tokens,
            tokens,
            P("dp", "seq"),
            P("dp", None, None),
            P("dp", None),
            vector,
            matrix,
            matrix,
            matrix,
            matrix,
            vector,
            vector,
            matrix,
            matrix,
            matrix,
            matrix,
            vector,
        ),
        out_specs=(
            tokens,
            tokens,
            vector,
            matrix,
            matrix,
            matrix,
            matrix,
            vector,
            vector,
            matrix,
            matrix,
            matrix,
            matrix,
            vector,
        ),
        check_vma=False,
    )
```

```python
import jax
import jax.numpy as jnp
from jax import lax
from jax.experimental import pallas as pl
from jax.experimental.pallas import tpu as pltpu
from jax.sharding import PartitionSpec as P

L_HEADS = 8
L_HEAD = 96
H_HEADS = 12
H_HEAD = 64
WINDOW = 128
LANES = 128

epsilon = 1e-06
masked_score = -1e30
gelu_scale = 0.7978845608028654
bf16 = jnp.bfloat16
f32 = jnp.float32


def dma_moves(index, arrays, out_shapes, moves):
    def body(index_ref, *refs):
        ins, outs, sems = refs[: len(arrays)], refs[len(arrays) : -1], refs[-1]
        copies = [
            pltpu.make_async_copy(source(ins, index_ref), target(outs, index_ref), sems.at[k])
            for k, (source, target) in enumerate(moves)
        ]
        for copy in copies:
            copy.start()
        for copy in copies:
            copy.wait()

    return pl.pallas_call(
        body,
        out_shape=[jax.ShapeDtypeStruct(s, a) for s, a in out_shapes],
        in_specs=[pl.BlockSpec(memory_space=pltpu.SMEM)]
        + [pl.BlockSpec(memory_space=pl.ANY)] * len(arrays),
        out_specs=[pl.BlockSpec(memory_space=pltpu.VMEM)] * len(out_shapes),
        scratch_shapes=[pltpu.SemaphoreType.DMA((len(moves),))],
        compiler_params=pltpu.CompilerParams(vmem_limit_bytes=16 * 2**20),
    )(index, *arrays)


def dp_stages(count):
    if count == 8:
        return [
            lambda i: i ^ (2 + 2 * (i & 1)),
            lambda i: i ^ (4 - 2 * (i & 1)),
            lambda i: i ^ 1,
        ]
    masks = [1 << b for b in range(count.bit_length() - 1)][::-1]
    return [lambda i, m=m: i ^ m for m in masks]


def dp_labels(count):
    labels = [()]
    for stage in range(len(dp_stages(count))):
        labels = labels + [label + (stage,) for label in labels]
    return labels


def dp_order():
    count, me = lax.axis_size("dp"), lax.axis_index("dp")
    stages = dp_stages(count)

    def source(label):
        at = me
        for stage in label[::-1]:
            at = stages[stage](at)
        return at

    return jnp.stack([source(label) for label in dp_labels(count)]).astype(jnp.int32)


def perm(count, stage):
    return [(i, stage(i)) for i in range(count)]


def perm_seq(count, k):
    return [(i, i ^ k) for i in range(count)]


def fence(*values):
    return lax.optimization_barrier(values) if len(values) > 1 else values


def gate(value, *others):
    return lax.optimization_barrier((value,) + others)[0] if others else value


def seq_order(steps):
    pos = lax.axis_index("seq")
    return jnp.stack([pos ^ k for k in steps]).astype(jnp.int32)


def place_seq(pieces, widths=None):
    return place(pieces, seq_order(range(len(pieces))), widths or [pieces[0].shape[-1]])


def place(pieces, order, widths):
    count, lead = len(pieces), pieces[0].shape[:-1]
    moves, shapes, low = [], [], 0
    for j, columns in enumerate(widths):
        shapes.append(((count,) + lead + (columns,), bf16))
        for k in range(count):
            moves.append(
                (
                    lambda ins, idx, k=k, low=low, columns=columns: ins[k].at[
                        ..., pl.ds(low, columns)
                    ],
                    lambda outs, idx, k=k, j=j: outs[j].at[idx[k]],
                )
            )
        low += columns
    return [p.reshape(-1, p.shape[-1]) for p in dma_moves(order, pieces, shapes, moves)]


def fold(block, rows):
    count, width = block.shape[-2:]
    extra = count - rows
    if not extra:
        return block
    if rows % 8 or extra % 8 or extra < 0 or rows % extra or width % (rows // extra * LANES):
        return block.reshape(block.shape[:-2] + (rows, -1))
    groups = jnp.split(block[..., rows:, :], rows // extra, axis=-1)
    return jnp.concatenate([block[..., :rows, :], jnp.concatenate(groups, axis=-2)], axis=-1)


def unfold(block, count, width):
    rows = block.shape[-2]
    extra = count - rows
    if not extra:
        return block
    if rows % 8 or extra % 8 or extra < 0 or rows % extra or width % (rows // extra * LANES):
        return block.reshape(block.shape[:-2] + (count, width))
    groups = jnp.split(block[..., width:], rows // extra, axis=-2)
    return jnp.concatenate([block[..., :width], jnp.concatenate(groups, axis=-1)], axis=-2)


def send_seq(piece_for, every=1):
    count = lax.axis_size("seq")
    steps = range(every, count, every)
    return [lax.ppermute(piece_for(k), "seq", perm_seq(count, k)) for k in steps]


def wave(pieces, hops, *after):
    count = lax.axis_size("dp")
    stages = dp_stages(count)
    for label in [p for p in pieces if len(p) == hops]:
        later = range(label[-1] + 1 if label else 0, len(stages))
        if len(later):
            pieces[label] = gate(pieces[label], *after)
        for stage in later:
            pieces[label + (stage,)] = lax.ppermute(
                pieces[label], "dp", perm(count, stages[stage])
            )


def place_dp(held, widths, *after):
    pieces = [held[label] for label in dp_labels(lax.axis_size("dp"))]
    return place(pieces, gate(dp_order(), *after), widths)


def scatter_dp(grads):
    count = lax.axis_size("dp")
    half = count // 2
    rows = grads[0].shape[1]
    width = sum(g.shape[2] for g in grads)
    moves, low = [], 0
    for j, grad in enumerate(grads):
        columns = grad.shape[2]
        for k in range(count):
            moves.append(
                (
                    lambda ins, idx, k=k, j=j: ins[j].at[idx[k]],
                    lambda outs, idx, k=k, low=low, columns=columns: outs[k // half].at[
                        k % half, :, pl.ds(low, columns)
                    ],
                )
            )
        low += columns
    shape = (half, rows, width)
    keep, send = dma_moves(dp_order(), grads, [(shape, bf16), (shape, bf16)], moves)
    return Scatter(keep, send)


class Scatter:
    def __init__(self, keep, send):
        self.keep, self.left = keep, dp_stages(lax.axis_size("dp"))
        self.hop(send)

    def hop(self, send):
        count = lax.axis_size("dp")
        self.got = lax.ppermute(send, "dp", perm(count, self.left.pop()))

    def step(self, *after):
        self.keep = gate(self.keep, *after)
        half = self.keep.shape[0] // 2
        wide = lambda part: part.astype(f32)
        send = (wide(self.keep[half:]) + wide(self.got[half:])).astype(bf16)
        self.keep = (wide(self.keep[:half]) + wide(self.got[:half])).astype(bf16)
        self.hop(send)

    def finish(self, *after):
        while len(self.left):
            self.step(*after)
        return gate(self.keep, *after)[0].astype(f32) + self.got[0].astype(f32)


def pick_seq(blocks):
    pos = lax.axis_index("seq")
    return lambda k: lax.dynamic_index_in_dim(blocks, pos ^ k, 0, keepdims=False)


class Sum:
    def __init__(self, part, *after, pair=False):
        self.masks = [1 << b for b in range(lax.axis_size("seq").bit_length() - 1)]
        if pair:
            self.masks = self.masks[:1]
        self.part = gate(part, *after)
        self.send()

    def send(self):
        pairs = perm_seq(lax.axis_size("seq"), self.masks.pop(0))
        self.got = lax.ppermute(self.part, "seq", pairs)

    def add(self, *after):
        part = gate(self.part, *after)
        self.part = (part.astype(f32) + self.got.astype(f32)).astype(bf16)
        if self.masks:
            self.send()

    def finish(self, *after):
        while self.masks:
            self.add(*after)
        self.add(*after)
        return self.part


def split_columns(odd, weights, chunk):
    rows, width = weights.shape
    pairs = width // (2 * chunk)

    def body(odd_ref, weights_ref, own_ref, other_ref):
        def copy(own, other):
            for j in range(pairs):
                at = pl.ds(j * chunk, chunk)
                own[:, at] = weights_ref[:, pl.ds(2 * j * chunk, chunk)]
                other[:, at] = weights_ref[:, pl.ds((2 * j + 1) * chunk, chunk)]

        @pl.when(odd_ref[0] == 0)
        def _():
            copy(own_ref, other_ref)

        @pl.when(odd_ref[0] == 1)
        def _():
            copy(other_ref, own_ref)

    return pl.pallas_call(
        body,
        in_specs=[pl.BlockSpec(memory_space=pltpu.SMEM), pl.BlockSpec(memory_space=pltpu.VMEM)],
        out_specs=[pl.BlockSpec(memory_space=pltpu.VMEM)] * 2,
        out_shape=[jax.ShapeDtypeStruct((rows, width // 2), weights.dtype)] * 2,
    )(odd, weights)


def join_columns(odd, pieces, chunk):
    rows, width = pieces[0].shape
    count = len(pieces)

    def body(odd_ref, *refs):
        out_ref = refs[-1]

        def fill(first, second):
            for j in range(width // chunk):
                at = pl.ds(j * chunk, chunk)
                for side, group in enumerate((first, second)):
                    total = group[0][:, at].astype(f32)
                    for ref in group[1:]:
                        total = total + ref[:, at].astype(f32)
                    out_ref[:, pl.ds((2 * j + side) * chunk, chunk)] = total

        @pl.when(odd_ref[0] == 0)
        def _():
            fill(refs[0:count:2], refs[1:count:2])

        @pl.when(odd_ref[0] == 1)
        def _():
            fill(refs[1:count:2], refs[0:count:2])

    return pl.pallas_call(
        body,
        in_specs=[pl.BlockSpec(memory_space=pltpu.SMEM)]
        + [pl.BlockSpec(memory_space=pltpu.VMEM)] * count,
        out_specs=pl.BlockSpec(memory_space=pltpu.VMEM),
        out_shape=jax.ShapeDtypeStruct((rows, 2 * width), f32),
    )(odd, *pieces)


def inv_rms(values):
    return lax.rsqrt(jnp.mean(values * values, axis=-1, keepdims=True) + epsilon)


def norm_back(values, inv, scaled):
    inner = jnp.mean(scaled * values, axis=-1, keepdims=True)
    return inv * scaled - values * (inv * inv * inv) * inner


def gelu_both(v):
    inner = jnp.tanh(gelu_scale * (v + 0.044715 * v * v * v))
    value = 0.5 * v * (1.0 + inner)
    slope = 0.5 * (1.0 + inner) + 0.5 * v * (1.0 - inner * inner) * gelu_scale * (
        1.0 + 3.0 * 0.044715 * v * v
    )
    return value, slope


def sigmoid(values):
    return 1.0 / (1.0 + jnp.exp(-values))


def dot(a, b):
    return lax.dot_general(a, b, (((1,), (0,)), ((), ())), preferred_element_type=f32)


def dot_nt(a, b):
    return lax.dot_general(a, b, (((1,), (1,)), ((), ())), preferred_element_type=f32)


def dot_tn(a, b):
    return lax.dot_general(a, b, (((0,), (0,)), ((), ())), preferred_element_type=f32)


def route_table(slots, count, token_pos):
    live = jnp.arange(slots.shape[0]) < count
    return ((slots[:, None] == token_pos[None, :]) & live[:, None]).astype(bf16)


def head_windows(width, head):
    found = []
    for low in range(0, width, head):
        first, last = low // LANES, (low + head - 1) // LANES
        found.append((first * LANES, (last + 1) * LANES, low - first * LANES))
    return found


def head_lanes(rows, low, high, offset, head):
    lane = lax.broadcasted_iota(jnp.int32, (rows, high - low), 1)
    return (lane >= offset) & (lane < offset + head)


def add_tiles(tiles, low, values):
    for t in range(values.shape[1] // LANES):
        part = values[:, t * LANES : (t + 1) * LANES]
        k = low // LANES + t
        tiles[k] = part if tiles[k] is None else tiles[k] + part


def attend(q, kv, q_seg, k_seg, head, block, reach, out_type):
    count, width = q.shape
    keys = kv.shape[0]
    span = block + 2 * reach if reach else keys
    windows = head_windows(width, head)
    scale = head ** (-0.5)

    def body(q_ref, kv_ref, q_seg_ref, k_seg_ref, out_ref, prob_ref):
        start = pl.multiple_of(pl.program_id(0) * block, block) if reach else 0
        rows = pl.ds(start, span)
        allowed = q_seg_ref[...] == k_seg_ref[:, rows]
        if reach:
            ahead = lax.broadcasted_iota(jnp.int32, (block, span), 1) - lax.broadcasted_iota(
                jnp.int32, (block, span), 0
            )
            allowed = allowed & (ahead >= 0) & (ahead <= 2 * reach)
        tiles = [None] * (width // LANES)
        for h, (low, high, offset) in enumerate(windows):
            mine = head_lanes(block, low, high, offset, head)
            q_head = jnp.where(mine, q_ref[:, low:high], 0)
            scores = dot_nt(q_head, kv_ref[rows, low:high]) * scale
            scores = jnp.where(allowed, scores, masked_score)
            raised = jnp.exp(scores - jnp.max(scores, axis=-1, keepdims=True))
            probs = (raised * (1.0 / jnp.sum(raised, axis=-1, keepdims=True))).astype(bf16)
            prob_ref[h] = probs
            mixed = dot(probs, kv_ref[rows, width + low : width + high])
            add_tiles(tiles, low, jnp.where(mine, mixed, 0.0))
        for t, tile in enumerate(tiles):
            out_ref[:, t * LANES : (t + 1) * LANES] = tile.astype(out_type)

    return pl.pallas_call(
        body,
        grid=(count // block,),
        in_specs=[
            pl.BlockSpec((block, width), lambda b: (b, 0)),
            pl.BlockSpec((keys, 2 * width), lambda b: (0, 0)),
            pl.BlockSpec((block, 1), lambda b: (b, 0)),
            pl.BlockSpec((1, keys), lambda b: (0, 0)),
        ],
        out_specs=[
            pl.BlockSpec((block, width), lambda b: (b, 0)),
            pl.BlockSpec((len(windows), block, span), lambda b: (0, b, 0)),
        ],
        out_shape=[
            jax.ShapeDtypeStruct((count, width), out_type),
            jax.ShapeDtypeStruct((len(windows), count, span), bf16),
        ],
        compiler_params=pltpu.CompilerParams(vmem_limit_bytes=32 * 2**20),
        cost_estimate=pl.CostEstimate(
            flops=4 * count * span * width,
            transcendentals=len(windows) * count * span,
            bytes_accessed=2 * (2 * count * width + 2 * keys * width + len(windows) * count * span),
        ),
    )(q, kv, q_seg[:, None], k_seg[None])


def attend_back(q, kv, probs, grad, head, block, reach):
    count, width = q.shape
    keys = kv.shape[0]
    span = block + 2 * reach if reach else keys
    windows = head_windows(width, head)
    scale = head ** (-0.5)

    def body(q_ref, kv_ref, prob_ref, grad_ref, q_grad_ref, kv_grad_ref, sums_ref):
        step = pl.program_id(0)

        @pl.when(step == 0)
        def _():
            sums_ref[...] = jnp.zeros_like(sums_ref)

        start = pl.multiple_of(step * block, block) if reach else 0
        rows = pl.ds(start, span)
        tiles = [None] * (width // LANES)
        for h, (low, high, offset) in enumerate(windows):
            mine = head_lanes(block, low, high, offset, head)
            q_head = jnp.where(mine, q_ref[:, low:high], 0)
            g_head = jnp.where(mine, grad_ref[:, low:high], 0)
            p_head = prob_ref[h]
            p_wide = p_head.astype(f32)
            p_grad = dot_nt(g_head, kv_ref[rows, width + low : width + high])
            inner = jnp.sum(p_wide * p_grad, axis=-1, keepdims=True)
            s_grad = (p_wide * (p_grad - inner)).astype(bf16)
            q_part = dot(s_grad, kv_ref[rows, low:high]) * scale
            add_tiles(tiles, low, jnp.where(mine, q_part, 0.0))
            sums_ref[rows, low:high] += dot_tn(s_grad, q_head) * scale
            sums_ref[rows, width + low : width + high] += dot_tn(p_head, g_head)
        for t, tile in enumerate(tiles):
            q_grad_ref[:, t * LANES : (t + 1) * LANES] = tile.astype(bf16)

        @pl.when(step == count // block - 1)
        def _():
            kv_grad_ref[...] = sums_ref[...].astype(bf16)

    return pl.pallas_call(
        body,
        grid=(count // block,),
        in_specs=[
            pl.BlockSpec((block, width), lambda b: (b, 0)),
            pl.BlockSpec((keys, 2 * width), lambda b: (0, 0)),
            pl.BlockSpec((len(windows), block, span), lambda b: (0, b, 0)),
            pl.BlockSpec((block, width), lambda b: (b, 0)),
        ],
        out_specs=[
            pl.BlockSpec((block, width), lambda b: (b, 0)),
            pl.BlockSpec((keys, 2 * width), lambda b: (0, 0)),
        ],
        out_shape=[
            jax.ShapeDtypeStruct((count, width), bf16),
            jax.ShapeDtypeStruct((keys, 2 * width), bf16),
        ],
        scratch_shapes=[pltpu.VMEM((keys, 2 * width), f32)],
        compiler_params=pltpu.CompilerParams(vmem_limit_bytes=40 * 2**20),
        cost_estimate=pl.CostEstimate(
            flops=8 * count * span * width,
            transcendentals=0,
            bytes_accessed=2 * (3 * count * width + 4 * keys * width + len(windows) * count * span),
        ),
    )(q, kv, probs, grad)


def shards(
    layer_input,
    cotangent,
    segment_ids,
    route_index,
    route_count,
    attn_gain,
    light_qkv,
    light_out,
    heavy_qkv,
    heavy_out,
    attn_router,
    ffn_gain,
    light_gate_up,
    light_down,
    heavy_gate_up,
    heavy_down,
    ffn_router,
):
    dp, seq = lax.axis_size("dp"), lax.axis_size("seq")
    pos = lax.axis_index("seq")
    x_in, cot, seg = layer_input[0], cotangent[0], segment_ids[0]
    tokens, width = x_in.shape
    slots, counts = route_index[0], route_count[0]
    routed = slots.shape[1]
    token_pos = pos * tokens + jnp.arange(tokens, dtype=jnp.int32)
    table_q = route_table(slots[0], counts[0], token_pos)
    table_kv = route_table(slots[1], counts[1], token_pos)
    table_f = route_table(slots[2], counts[2], token_pos)

    rows, wide = light_qkv.shape
    unit, light_unit = heavy_down.shape[0], light_down.shape[0]
    light_cut, half = light_gate_up.shape[1], seq // 2
    merged = lambda block: block.reshape(-1, block.shape[-1])
    by_dp = lambda grad: grad.reshape(dp, -1, grad.shape[1])
    by_seq = lambda mine: mine.reshape(seq, rows, -1)
    hops = len(dp_stages(dp))
    odd = pos & 1
    fold_width = width * light_unit // rows

    small = jnp.stack([attn_gain, attn_router, ffn_gain, ffn_router], axis=1)
    first = jnp.concatenate([light_qkv, jnp.pad(small, ((0, 0), (0, LANES - 4)))], axis=1)
    got_first = send_seq(lambda k: first)
    light_ffn_own = jnp.concatenate([light_gate_up, fold(light_down, rows)], axis=1)
    light_ffn_all = lax.all_gather(light_ffn_own, ("dp", "seq"), axis=0, tiled=True)
    marked = jnp.concatenate(
        [x_in, jnp.broadcast_to(seg.astype(bf16)[:, None], (tokens, LANES))], axis=1
    )
    left = lax.ppermute(marked[tokens - WINDOW :], "seq", [(i, i + 1) for i in range(seq - 1)])
    right = lax.ppermute(marked[:WINDOW], "seq", [(i + 1, i) for i in range(seq - 1)])
    kv_part = dot(table_kv, marked).astype(bf16)
    own_gu, other_gu = split_columns(odd[None], heavy_gate_up, unit)
    first_held = {(): place_seq([first] + got_first)[0]}
    wave(first_held, 0)

    others = fence(heavy_qkv, light_out, heavy_out, *got_first)[:3]
    second = jnp.concatenate(others, axis=1)
    sum_kv = Sum(kv_part, *got_first)
    got_second = send_seq(lambda k: second)
    for h in range(1, hops):
        wave(first_held, h, second)
    w_lqkv, small_all = place_dp(first_held, [wide, LANES])

    small_t = small_all[:, :4].T
    gain_attn = small_t[0].astype(f32)[None]
    router_attn = small_t[1][None]
    gain_ffn = small_t[2].astype(f32)[None]
    router_ffn = small_t[3][None]

    ext_marked = jnp.concatenate([left, marked, right], axis=0)
    ext_in = ext_marked[:, :width].astype(f32)
    ext_inv = inv_rms(ext_in)
    normed_ext = (ext_in * ext_inv * gain_attn).astype(bf16)
    normed = normed_ext[WINDOW : WINDOW + tokens]
    place_of = jnp.arange(tokens + 2 * WINDOW) - WINDOW
    outside = ((pos == 0) & (place_of < 0)) | ((pos == seq - 1) & (place_of >= tokens))
    key_seg = jnp.where(outside, -1.0, ext_marked[:, width].astype(f32))
    seg_f = seg.astype(f32)
    light_q = dot(normed, w_lqkv[:, :width]).astype(bf16)
    light_kv = dot(normed_ext, w_lqkv[:, width:]).astype(bf16)
    cot_part = dot(table_f, cot).astype(bf16)

    (second_z,) = place_seq([gate(second, light_kv, light_q)] + got_second)
    second_held = {(): second_z}
    wave(second_held, 0)
    sum_kv.add()
    light_mixed, light_probs = attend(
        gate(light_q, second_z), light_kv, seg_f, key_seg, L_HEAD, WINDOW, WINDOW, bf16
    )
    q_rows = dot(table_q, normed).astype(bf16)
    q_seg = jnp.sum(table_q.astype(f32) * seg_f[None], axis=1)

    for h in range(1, hops):
        wave(second_held, h, light_mixed)
    kv_marked = sum_kv.finish(light_mixed)
    own_gu, other_gu = fence(own_gu, other_gu, light_mixed)[:2]
    got_gu = send_seq(lambda k: other_gu if k & 1 else own_gu)
    got_down = send_seq(lambda k: gate(heavy_down, light_mixed), 2)
    w_hqkv, w_lout, w_hout = place_dp(second_held, [wide, width, width], light_mixed)
    kv_in = kv_marked[:, :width].astype(f32)
    kv_rows = (kv_in * inv_rms(kv_in) * gain_attn).astype(bf16)
    kv_seg = jnp.where(jnp.arange(routed) < counts[1], kv_marked[:, width].astype(f32), -1.0)
    heavy_q = dot(q_rows, w_hqkv[:, :width]).astype(bf16)
    heavy_kv = dot(kv_rows, w_hqkv[:, width:]).astype(bf16)
    heavy_mixed, heavy_probs = attend(
        heavy_q, heavy_kv, q_seg, kv_seg, H_HEAD, min(routed, 256), 0, f32
    )
    gate_attn = sigmoid(
        jnp.sum(q_rows.astype(f32) * router_attn.astype(f32), axis=1, keepdims=True)
    )
    gated = (gate_attn * heavy_mixed).astype(bf16)
    heavy_rows = dot(gated, w_hout).astype(bf16)
    midway = x_in.astype(f32) + dot(light_mixed, w_lout) + dot_tn(table_q, heavy_rows)
    inv_ffn = inv_rms(midway)
    normed_ffn = (midway * inv_ffn * gain_ffn).astype(bf16)
    rows_part = dot(table_f, normed_ffn).astype(bf16)

    sum_rows = Sum(rows_part, pair=True)
    sum_cot = Sum(cot_part, rows_part, pair=True)
    (gu_z,) = place_seq([gate(own_gu, heavy_mixed)] + got_gu)
    (down_z,) = place([gate(heavy_down, heavy_mixed)] + got_down, seq_order(range(0, seq, 2)) // 2, [width])
    gu_held, down_held = {(): gu_z}, {(): down_z}
    wave(gu_held, 0)
    wave(down_held, 0)
    w_lgu = light_ffn_all[:, :light_cut]
    w_ldown = merged(unfold(light_ffn_all[:, light_cut:].reshape(dp * seq, rows, -1), light_unit, width))

    light_units = w_ldown.shape[0]
    light_pre = dot(normed_ffn, w_lgu)
    light_gate, light_up = light_pre[:, :light_units], light_pre[:, light_units:]
    light_act, light_slope = gelu_both(light_gate)
    light_hidden = (light_act * light_up).astype(bf16)
    light_ffn = dot(light_hidden, w_ldown)
    grad_ldown = dot_tn(light_hidden, cot).astype(bf16)
    hidden_grad = dot_nt(cot, w_ldown).astype(bf16).astype(f32)
    light_pre_grad = jnp.concatenate(
        [hidden_grad * light_up * light_slope, hidden_grad * light_act], axis=-1
    ).astype(bf16)
    grad_lgu = dot_tn(normed_ffn, light_pre_grad).astype(bf16)
    normed_ffn_grad = dot_nt(light_pre_grad, w_lgu)

    grad_ldown = merged(fold(grad_ldown.reshape(dp * seq, -1, width), rows))
    light_grads = jnp.concatenate([grad_lgu, grad_ldown], axis=1)
    light_sum = lax.psum_scatter(light_grads, ("dp", "seq"), scatter_dimension=0, tiled=True)
    for h in range(1, hops):
        wave(gu_held, h, light_ffn)
        wave(down_held, h, light_ffn)
    ffn_rows = sum_rows.finish(normed_ffn_grad, light_ffn, light_grads)
    cot_rows = sum_cot.finish(normed_ffn_grad, light_ffn)
    (w_hgu,) = place_dp(gu_held, [gu_z.shape[1]], ffn_rows)
    (w_hdown,) = place_dp(down_held, [width], ffn_rows)

    heavy_units = w_hdown.shape[0]
    heavy_pre = dot(ffn_rows, w_hgu)
    heavy_gate, heavy_up = heavy_pre[:, :heavy_units], heavy_pre[:, heavy_units:]
    heavy_act, heavy_slope = gelu_both(heavy_gate)
    ffn_gate = sigmoid(
        jnp.sum(ffn_rows.astype(f32) * router_ffn.astype(f32), axis=1, keepdims=True)
    )
    heavy_hidden = (ffn_gate * heavy_act * heavy_up).astype(bf16)
    heavy_grad = dot_nt(cot_rows, w_hdown).astype(bf16).astype(f32)
    heavy_pre_grad = jnp.concatenate(
        [heavy_grad * ffn_gate * heavy_up * heavy_slope, heavy_grad * ffn_gate * heavy_act],
        axis=-1,
    ).astype(bf16)
    ffn_score_grad = (
        ffn_gate
        * (1.0 - ffn_gate)
        * jnp.sum(heavy_grad * heavy_act * heavy_up, axis=1, keepdims=True)
    )
    rows_grad_part = dot_nt(heavy_pre_grad, w_hgu) + ffn_score_grad * router_ffn.astype(f32)
    rows_grad = rows_grad_part.astype(bf16)
    sum_rows = Sum(rows_grad, pair=True)
    heavy_hidden, heavy_pre_grad, ffn_score_grad = fence(
        heavy_hidden, heavy_pre_grad, ffn_score_grad, rows_grad
    )[:3]
    grad_ffn_router = jnp.sum(ffn_rows.astype(f32) * ffn_score_grad, axis=0)
    grad_hdown = dot_tn(heavy_hidden, cot_rows).astype(bf16)
    grad_hgu = dot_tn(ffn_rows, heavy_pre_grad).astype(bf16)
    out_part = dot(heavy_hidden, w_hdown).astype(bf16)
    rows_grad = sum_rows.finish(grad_hdown, grad_hgu, out_part)
    sum_heavy = [scatter_dp([by_dp(grad_hgu)]), scatter_dp([by_dp(grad_hdown)])]

    sum_out = Sum(out_part, rows_grad, pair=True)
    normed_ffn_grad = normed_ffn_grad + dot_tn(table_f, rows_grad)
    midway_grad = cot.astype(f32) + norm_back(midway, inv_ffn, normed_ffn_grad * gain_ffn)

    out_grad = midway_grad.astype(bf16)
    for s in sum_heavy:
        s.step(out_grad)
    out_grad = gate(out_grad, *[s.keep for s in sum_heavy])
    grad_lout = dot_tn(light_mixed, out_grad).astype(bf16)
    heavy_out_cot = dot(table_q, out_grad).astype(bf16)
    grad_hout = dot_tn(gated, heavy_out_cot).astype(bf16)
    gated_grad = dot_nt(heavy_out_cot, w_hout).astype(bf16).astype(f32)
    heavy_mixed_grad = (gate_attn * gated_grad).astype(bf16)
    attn_score_grad = gate_attn * (1.0 - gate_attn) * jnp.sum(gated_grad * heavy_mixed, axis=1, keepdims=True)
    heavy_q_grad, heavy_kv_grad = attend_back(
        heavy_q, heavy_kv, heavy_probs, heavy_mixed_grad, H_HEAD, min(routed, 256), 0
    )
    grad_hq = dot_tn(q_rows, heavy_q_grad).astype(bf16)
    grad_hkv = dot_tn(kv_rows, heavy_kv_grad).astype(bf16)
    grad_attn_router = jnp.sum(q_rows.astype(f32) * attn_score_grad, axis=0)
    routers = jnp.pad(
        jnp.stack([grad_attn_router, grad_ffn_router], axis=1), ((0, 0), (0, LANES - 2))
    ).astype(bf16)
    q_rows_grad = (
        dot_nt(heavy_q_grad, w_hqkv[:, :width]) + attn_score_grad * router_attn.astype(f32)
    ).astype(bf16)
    kv_send = dot_nt(heavy_kv_grad, w_hqkv[:, width:]).astype(bf16)
    mixed_grad = dot_nt(out_grad, w_lout).astype(bf16)
    attn_grads = [by_dp(g) for g in (grad_hq, grad_hkv, grad_lout, grad_hout, routers)]

    sum_attn = scatter_dp(attn_grads)
    sum_kv = Sum(kv_send)
    out_part = sum_out.finish(kv_send)
    for s in sum_heavy:
        s.step(kv_send)
    light_q_grad, light_kv_grad = attend_back(
        light_q,
        light_kv,
        light_probs,
        gate(mixed_grad, sum_attn.keep),
        L_HEAD,
        WINDOW,
        WINDOW,
    )

    sum_attn.step(light_kv_grad)
    grad_lq = by_dp(dot_tn(normed, light_q_grad).astype(bf16))
    grad_lkv = by_dp(dot_tn(normed_ext, light_kv_grad).astype(bf16))
    sum_last = scatter_dp([grad_lq, grad_lkv])
    heavy_z = by_seq(sum_heavy[0].finish(sum_last.keep)).astype(bf16)
    down_z = sum_heavy[1].finish(sum_last.keep).astype(bf16).reshape(half, unit, width)
    sum_kv.add(grad_lkv)
    got_heavy = [pick_seq(heavy_z)(0)] + send_seq(pick_seq(heavy_z))
    pick_down = lambda k: lax.dynamic_index_in_dim(down_z, (pos ^ k) // 2, 0, keepdims=False)
    got_down = [pick_down(0)] + send_seq(pick_down, 2)
    sum_last.step()
    ext_grad = dot_nt(gate(light_kv_grad, sum_last.keep), w_lqkv[:, width:])
    from_right = lax.ppermute(
        ext_grad[WINDOW + tokens :].astype(bf16), "seq", [(i, i + 1) for i in range(seq - 1)]
    )
    from_left = lax.ppermute(
        ext_grad[:WINDOW].astype(bf16), "seq", [(i + 1, i) for i in range(seq - 1)]
    )
    own_grad = (
        ext_grad[WINDOW : WINDOW + tokens]
        + dot_nt(light_q_grad, w_lqkv[:, :width])
        + dot_tn(table_q, q_rows_grad)
    )
    sum_last.step(own_grad)
    sum_attn.step(own_grad)
    attn_mine = by_seq(sum_attn.finish(own_grad))
    light_last = by_seq(sum_last.finish(attn_mine))
    attn_sent = send_seq(pick_seq(attn_mine.astype(bf16)))
    light_sent = send_seq(pick_seq(light_last.astype(bf16)))
    attn_outs = pick_seq(attn_mine)(0) + sum(g.astype(f32) for g in attn_sent)
    last_mine = light_last
    light_last = light_sent[0]
    kv_total = sum_kv.finish(light_last)
    light_outs = pick_seq(last_mine)(0) + sum(g.astype(f32) for g in light_sent)

    light_sum = gate(light_sum, light_last, ext_grad).astype(f32)
    out_light_gate_up = light_sum[:, :light_cut]
    out_light_down = unfold(light_sum[:, light_cut:], light_unit, width)
    got_heavy = [gate(g, light_last) for g in got_heavy]
    got_down = [gate(g, light_last) for g in got_down]
    out_heavy_down = sum(g.astype(f32) for g in got_down)
    out_heavy_gate_up = join_columns(odd[None], got_heavy, unit)
    midway, out_part = fence(midway, out_part, light_last)[:2]
    layer_output = (midway + light_ffn + dot_tn(table_f, out_part)).astype(bf16)
    out_heavy_qkv = attn_outs[:, :wide]
    out_light_out = attn_outs[:, wide : wide + width]
    out_heavy_out = attn_outs[:, wide + width : wide + 2 * width]
    out_attn_router = attn_outs[:, wide + 2 * width]
    out_ffn_router = attn_outs[:, wide + 2 * width + 1]

    def along(weight, grad):
        return jnp.sum(weight.astype(f32) * grad, axis=1)

    out_attn_gain = (
        along(light_qkv, light_outs)
        + along(heavy_qkv, out_heavy_qkv)
        + attn_router.astype(f32) * out_attn_router
    ) / attn_gain.astype(f32)
    out_ffn_gain = (
        along(light_gate_up, out_light_gate_up)
        + along(heavy_gate_up, out_heavy_gate_up)
        + ffn_router.astype(f32) * out_ffn_router
    ) / ffn_gain.astype(f32)
    edge = jnp.concatenate(
        [from_right.astype(f32), jnp.zeros((tokens - 2 * WINDOW, width), f32), from_left.astype(f32)]
    )
    total_grad = own_grad + edge + dot_tn(table_kv, kv_total)
    x_wide = x_in.astype(f32)
    input_grad = midway_grad + norm_back(
        x_wide, ext_inv[WINDOW : WINDOW + tokens], total_grad * gain_attn
    )

    return (
        layer_output[None],
        input_grad.astype(bf16)[None],
        out_attn_gain,
        light_outs,
        out_light_out,
        out_heavy_qkv,
        out_heavy_out,
        out_attn_router,
        out_ffn_gain,
        out_light_gate_up,
        out_light_down,
        out_heavy_gate_up,
        out_heavy_down,
        out_ffn_router,
    )


def solution(mesh):
    both = ("dp", "seq")
    vector, matrix, tokens = P(both), P(both, None), P("dp", "seq", None)
    return jax.shard_map(
        shards,
        mesh=mesh,
        in_specs=(
            tokens,
            tokens,
            P("dp", "seq"),
            P("dp", None, None),
            P("dp", None),
            vector,
            matrix,
            matrix,
            matrix,
            matrix,
            vector,
            vector,
            matrix,
            matrix,
            matrix,
            matrix,
            vector,
        ),
        out_specs=(
            tokens,
            tokens,
            vector,
            matrix,
            matrix,
            matrix,
            matrix,
            vector,
            vector,
            matrix,
            matrix,
            matrix,
            matrix,
            vector,
        ),
        check_vma=False,
    )
```
